32 devices in a mesh: enc: 4 (over x, core), row: 4 (over z), col: 2 (over y).
Axes of the slice: x: 2, y: 2, z: 4, core: 2. Of those that a mesh axis runs over, the one named last changes fastest.
Arguments:
- out_grad: bfloat16 [48, 8192], P(None, ('enc', 'col')), may hold values from -6 to 6
- gate_pre: bfloat16 [48, 29568], P('enc', 'row'), may hold values from -6 to 6
- up_pre: bfloat16 [48, 29568], P('enc', 'row'), may hold values from -6 to 6
- w_gate: bfloat16 [8192, 29568], P(('enc', 'col'), 'row'), may hold values from -0.0625 to 0.0625
- w_up: bfloat16 [8192, 29568], P(('enc', 'col'), 'row'), may hold values from -0.0625 to 0.0625
- w_down: bfloat16 [29568, 8192], P('row', ('enc', 'col')), may hold values from -0.03125 to 0.03125
- w_proj: bfloat16 [12800, 8192], P(None, ('enc', 'col')), may hold values from -0.0546875 to 0.0546875
- enc_hidden: bfloat16 [192, 6400], P('row', ('enc', 'col')), may hold values from -6 to 6
- route: int32 [48], replicated, may hold values from 0 to 47, each once
- img_count: int32 [4], replicated, may hold values from 1 to 12
Outputs:
- enc_grad: bfloat16 [3200, 6400], P(None, ('enc', 'col'))
The draws below stay inside these ranges and needn't reach their ends.
Inputs may be any that keep to these rules, and one draw needn't show every extreme that they name: route[12 * r + k] is the language row that holds slot k of row group r; every language row appears once. Slots k of row group r with k >= img_count[r] are empty.
All inputs are finite; a program needn't handle non-finite values.
Results may differ from the reference program's by a relative error of at most 0.02.
Values may be sent and summed in bfloat16 or wider, within the bound.
No kernel may reach another device: no remote copies, remote signals or barrier semaphores. Data moves between devices by JAX's collectives and lax.ppermute only.
A program may use at most 128 MiB of HBM per device.

```python
import math
import jax
import jax.numpy as jnp
from jax import lax

D = 8192
FF = 29568
VD = 3200
VF = 6400
SHUF = 4
IMG = 12
NI = 48
PATCH = 192
PD = 12800
N_ROW = 4


def plant(values, rng, low, top_value):
    dims = values.shape
    index_at = [jax.random.randint(jax.random.fold_in(rng, axis), (), 0, dims[axis]) for axis in range(len(dims))]
    values = values.at[tuple(index_at)].set(low)
    longest = dims.index(max(dims))
    index_at[longest] = (index_at[longest] + 1) % dims[longest]
    return values.at[tuple(index_at)].set(top_value)


def block_scale(own_key, extent, cuts, low, largest):
    def one(dim, blocks):
        draws = jax.random.uniform(jax.random.fold_in(jax.random.fold_in(own_key, 6), dim), (blocks,), jnp.float32, low / len(cuts), largest / len(cuts))
        return jnp.repeat(jnp.exp(draws), extent[dim] // blocks).reshape((-1,) + (1,) * (len(extent) - dim - 1))

    level = one(*cuts[0])
    for cut in cuts[1:]:
        level = level * one(*cut)
    return level


def bell_draw(rng, extent, spread, limit, pieces=(), kind=jnp.bfloat16):
    level = block_scale(rng, extent, pieces, -0.22, 0.18) if pieces else 1.0
    result = jax.random.normal(rng, extent, jnp.float32) * spread * level
    return jnp.minimum(jnp.maximum(result, -limit), limit).astype(kind)


def setup_inputs(seed: int = 0) -> dict:
    splits = jax.random.split(jax.random.key(seed), 11)
    out_grad = bell_draw(splits[0], (NI, D), 1.0, 6.0, ((1, 8),))
    gate_pre = bell_draw(splits[1], (NI, FF), 1.0, 6.0, ((0, 4), (1, 4)))
    up_pre = bell_draw(splits[2], (NI, FF), 1.0, 6.0, ((0, 4), (1, 4)))
    w_gate = bell_draw(splits[3], (D, FF), D ** -0.5, 0.0625, ((0, 8), (1, 4)))
    w_up = bell_draw(splits[4], (D, FF), D ** -0.5, 0.0625, ((0, 8), (1, 4)))
    w_down = bell_draw(splits[5], (FF, D), FF ** -0.5, 0.03125, ((0, 4), (1, 8)))
    w_proj = bell_draw(splits[6], (PD, D), PD ** -0.5, 0.0546875, ((1, 8),))
    enc_hidden = bell_draw(splits[7], (PATCH, VF), 1.0, 6.0, ((0, 4), (1, 8)))
    route = jax.random.permutation(splits[8], NI).astype(jnp.int32)
    img_count = plant(jax.random.randint(splits[9], (N_ROW,), 1, IMG + 1), jax.random.fold_in(splits[9], 1), 1, IMG).astype(jnp.int32)
    return {"out_grad": out_grad, "gate_pre": gate_pre, "up_pre": up_pre, "w_gate": w_gate, "w_up": w_up, "w_down": w_down, "w_proj": w_proj, "enc_hidden": enc_hidden, "route": route, "img_count": img_count}


def reference(out_grad, gate_pre, up_pre, w_gate, w_up, w_down, w_proj, enc_hidden, route, img_count):
    hidden_grad = jnp.dot(out_grad, w_down.T, preferred_element_type=jnp.float32)
    gate_vals = gate_pre.astype(jnp.float32)
    up_vals = up_pre.astype(jnp.float32)
    squash = jax.nn.sigmoid(gate_vals)
    grad_gate = (hidden_grad * up_vals * squash * (1.0 + gate_vals * (1.0 - squash))).astype(jnp.bfloat16)
    grad_up = (hidden_grad * gate_vals * squash).astype(jnp.bfloat16)
    routed_gate = jnp.take(grad_gate, route, axis=0)
    routed_up = jnp.take(grad_up, route, axis=0)
    input_grad = jnp.dot(routed_gate, w_gate.T, preferred_element_type=jnp.float32) + jnp.dot(routed_up, w_up.T, preferred_element_type=jnp.float32)
    positions = jnp.arange(NI, dtype=jnp.int32)
    alive_mask = positions % IMG < jnp.repeat(img_count, IMG)
    image_grad = jnp.where(alive_mask[:, None], input_grad, jnp.zeros_like(input_grad)).astype(jnp.bfloat16)
    shuffled_grad = jnp.dot(image_grad, w_proj.T, preferred_element_type=jnp.float32)
    patch_grad = shuffled_grad.reshape(NI, VD, SHUF).transpose(0, 2, 1).reshape(PATCH, VD).astype(jnp.bfloat16)
    hidden_groups = enc_hidden.reshape(N_ROW, SHUF * IMG, VF)
    grad_groups = patch_grad.reshape(N_ROW, SHUF * IMG, VD)
    scale = 1.0 / math.sqrt(PATCH)

    def add_group(total, pair):
        term = lax.dot_general(pair[1], pair[0], (((0,), (0,)), ((), ())), preferred_element_type=jnp.float32) * scale
        rounded = lax.optimization_barrier(term.astype(jnp.bfloat16))
        return (total + rounded.astype(jnp.float32), None)
    total, unused = lax.scan(add_group, jnp.zeros((VD, VF), jnp.float32), (hidden_groups, grad_groups))
    return total.astype(jnp.bfloat16)
```

```python
import functools
import math

import jax
import jax.numpy as jnp
from jax import lax
from jax.experimental import pallas as pl
from jax.experimental.pallas import tpu as pltpu
from jax.sharding import PartitionSpec as P

SHUF = 4
CORES = 2
LANES = 128
AXES = ("enc", "row", "col")
BF = jnp.bfloat16
F32 = jnp.float32


def cdiv(a, b):
    return -(-a // b)


def dot_nt(left, right):
    return lax.dot_general(left, right, (((1,), (1,)), ((), ())), preferred_element_type=F32)


def dot_nn(left, right):
    return lax.dot_general(left, right, (((1,), (0,)), ((), ())), preferred_element_type=F32)


def dot_tn(left, right):
    return lax.dot_general(left, right, (((0,), (0,)), ((), ())), preferred_element_type=F32)


class Grid:
    def __init__(self):
        self.enc, self.rows, self.cols = (lax.axis_size(a) for a in AXES)
        self.xs = self.enc // CORES
        self.chips = self.xs * self.cols
        enc = lax.axis_index("enc")
        self.core = enc % CORES
        self.x = enc // CORES
        self.y = lax.axis_index("col")
        self.z = lax.axis_index("row")
        self.shifts = [(dx, dy) for dx in range(self.xs) for dy in range(self.cols)]

    def send(self, value, dx=0, dy=0, core=0, row=None):
        pairs = []
        for e in range(self.enc):
            for r in range(self.rows):
                for c in range(self.cols):
                    x, k = divmod(e, CORES)
                    target = (((x + dx) % self.xs) * CORES + (k ^ core), r if row is None else row(r), (c + dy) % self.cols)
                    flat = [(a * self.rows + b) * self.cols + d for a, b, d in ((e, r, c), target)]
                    pairs.append(tuple(flat))
        return lax.ppermute(value, AXES, pairs)

    def swap(self, value):
        return self.send(value, core=1)


def shuffle_matmul(image_grad, w_proj, first, steps):
    slots, width = image_grad.shape
    half = slots // CORES
    block = SHUF * LANES
    last = cdiv(w_proj.shape[0], block) - 1

    def kernel(first_ref, grad_ref, w_ref, out_ref, order):
        @pl.when(pl.program_id(0) == 0)
        def _():
            source = lax.broadcasted_iota(jnp.int32, (block, block), 0)
            target = lax.broadcasted_iota(jnp.int32, (block, block), 1)
            order[...] = jnp.where(source == SHUF * (target % LANES) + target // LANES, 1.0, 0.0).astype(BF)

        part = dot_nt(grad_ref[...], w_ref[...]).astype(BF)
        part = dot_nn(part, order[...]).astype(BF)
        for core in range(CORES):
            for q in range(SHUF):
                out_ref[core, q] = part[core * half : (core + 1) * half, q * LANES : (q + 1) * LANES]

    return pl.pallas_call(
        kernel,
        out_shape=jax.ShapeDtypeStruct((CORES, SHUF, half, steps * LANES), BF),
        grid_spec=pltpu.PrefetchScalarGridSpec(
            num_scalar_prefetch=1,
            grid=(steps,),
            in_specs=[
                pl.BlockSpec((slots, width), lambda i, first: (0, 0)),
                pl.BlockSpec((block, width), lambda i, first: (jnp.minimum(first[0] + i, last), 0)),
            ],
            out_specs=pl.BlockSpec((CORES, SHUF, half, LANES), lambda i, first: (0, 0, 0, i)),
            scratch_shapes=[pltpu.VMEM((block, block), BF)],
        ),
        cost_estimate=pl.CostEstimate(
            flops=2 * slots * width * block * steps, bytes_accessed=2 * width * block * steps, transcendentals=0
        ),
        name="shuffle_matmul",
    )(first, image_grad, w_proj)


def weight_grad(patches, hidden, where, features, scale):
    count, patch, block = patches.shape
    units = hidden.shape[1]

    def kernel(where_ref, patch_ref, hidden_ref, out_ref):
        out_ref[...] = (dot_tn(hidden_ref[...], patch_ref[0]) * scale).astype(BF)

    return pl.pallas_call(
        kernel,
        out_shape=jax.ShapeDtypeStruct((units, features), BF),
        grid_spec=pltpu.PrefetchScalarGridSpec(
            num_scalar_prefetch=1,
            grid=(count,),
            in_specs=[
                pl.BlockSpec((1, patch, block), lambda i, where: (i, 0, 0)),
                pl.BlockSpec((patch, units), lambda i, where: (0, 0)),
            ],
            out_specs=pl.BlockSpec((units, block), lambda i, where: (0, where[i])),
        ),
        cost_estimate=pl.CostEstimate(
            flops=2 * count * patch * block * units, bytes_accessed=2 * units * features, transcendentals=0
        ),
        name="weight_grad",
    )(where, patches, hidden)


def gather_rows(g, value):
    stack = value[None]
    if g.rows & (g.rows - 1):
        return lax.all_gather(value, "row", axis=0, tiled=False)
    for mask in row_masks(g):
        stack = jnp.concatenate([stack, g.send(stack, row=lambda r: r ^ mask)])
    return stack


def row_masks(g):
    return [2 ** (s + 1) - 1 for s in range(g.rows.bit_length() - 1)]


def row_order(g):
    if g.rows & (g.rows - 1):
        return jnp.arange(g.rows, dtype=jnp.int32)
    order = [0]
    for mask in row_masks(g):
        order = order + [o ^ mask for o in order]
    return jnp.array(order, jnp.int32) ^ g.z


def sum_rows(g, value):
    if g.rows & (g.rows - 1):
        return lax.psum(value.astype(F32), "row").astype(BF)
    for mask in row_masks(g):
        value = (value.astype(F32) + g.send(value, row=lambda r: r ^ mask).astype(F32)).astype(BF)
    return value


def shards(out_grad, gate_pre, up_pre, w_gate, w_up, w_down, w_proj, enc_hidden, route, img_count):
    g = Grid()
    slots = route.shape[0]
    own = gate_pre.shape[0]
    half = slots // CORES
    units = w_down.shape[0]
    share = cdiv(cdiv(units, g.cols), LANES) * LANES
    padded = share * g.cols

    hidden = dot_nt(out_grad, w_down)
    hidden = jnp.pad(hidden, ((0, 0), (0, padded - units)))
    hidden = hidden.reshape(g.xs, CORES, own, g.cols, share).transpose(3, 1, 0, 2, 4)

    def core_part(a, core):
        return lax.dynamic_index_in_dim(a, core, 1, keepdims=False)

    other = g.swap(core_part(hidden.astype(BF), 1 - g.core))
    mine = core_part(hidden, g.core) + other.astype(F32)
    def for_chip(a, dx, dy):
        a = lax.dynamic_index_in_dim(a, (g.y + dy) % g.cols, 0, keepdims=False)
        return lax.dynamic_index_in_dim(a, (g.x + dx) % g.xs, 0, keepdims=False)

    narrow = mine.astype(BF)
    total = for_chip(mine, 0, 0)
    for dx, dy in g.shifts[1:]:
        total = total + g.send(for_chip(narrow, dx, dy), dx=dx, dy=dy).astype(F32)

    def my_share(a):
        a = jnp.pad(a, ((0, 0), (0, padded - units)))
        return lax.dynamic_slice_in_dim(a, g.y * share, share, 1).astype(F32)

    gate, up = my_share(gate_pre), my_share(up_pre)
    squash = jax.nn.sigmoid(gate)
    grads = jnp.stack([total * up * squash * (1.0 + gate * (1.0 - squash)), total * gate * squash]).astype(BF)
    pieces = jnp.stack([grads] + [g.send(grads, dx=dx, dy=dy) for dx, dy in g.shifts[1:]])
    pieces = jnp.stack([pieces, g.swap(pieces)])
    pieces = pieces.reshape(CORES, g.xs, g.cols, 2, own, share)
    flipped = jnp.flip(pieces, 2)
    pieces = jnp.where(g.y == 0, pieces, flipped) if g.cols == 2 else jnp.roll(flipped, g.y + 1, axis=2)
    pieces = pieces.transpose(3, 0, 1, 4, 2, 5).reshape(2, slots, padded)[:, :, :units]
    input_part = dot_nt(pieces[0], w_gate) + dot_nt(pieces[1], w_up)

    image = slots // g.rows
    chip, local = route // own, route % own
    x, core = chip // CORES, chip % CORES
    place = ((core ^ g.core) * g.xs + (g.x - x) % g.xs) * own + local
    positions = jnp.arange(slots, dtype=jnp.int32)
    alive = positions % image < jnp.repeat(img_count, image)
    place = jnp.where(alive, place, -1)
    pick = (place[:, None] == positions[None, :]).astype(BF)
    image_grad = dot_nn(pick, input_part.astype(BF)).astype(BF)
    image_grad = sum_rows(g, image_grad)

    features = w_proj.shape[0] // SHUF
    steps = cdiv(cdiv(features, g.rows), LANES)
    shuffled = shuffle_matmul(image_grad, w_proj, (g.z * steps).reshape(1), steps)
    wide = steps * LANES
    keep = lax.dynamic_index_in_dim(shuffled, g.core, 0, keepdims=False)
    give = lax.dynamic_index_in_dim(shuffled, 1 - g.core, 0, keepdims=False)
    mine = (keep.astype(F32) + g.swap(give).astype(F32)).reshape(g.chips, SHUF * half // g.chips, wide)
    narrow = mine.astype(BF)

    def chip_part(a, dx, dy):
        index = ((g.x + dx) % g.xs) * g.cols + (g.y + dy) % g.cols
        return lax.dynamic_index_in_dim(a, index, 0, keepdims=False)

    total = chip_part(mine, 0, 0)
    for dx, dy in g.shifts[1:]:
        total = total + g.send(chip_part(narrow, dx, dy), dx=dx, dy=dy).astype(F32)
    patch_grad = total.astype(BF)
    patch_grad = jnp.concatenate([patch_grad] + [g.send(patch_grad, dx=dx, dy=dy) for dx, dy in g.shifts[1:]])
    patch_grad = gather_rows(g, patch_grad)
    patch_grad = jnp.concatenate([patch_grad, g.swap(patch_grad)], axis=1)

    all_hidden = gather_rows(g, enc_hidden)
    group = enc_hidden.shape[0]
    patches = group * g.rows
    piece = SHUF * half // g.chips
    spot = jnp.arange(patches, dtype=jnp.int32)
    core = (spot // (g.chips * piece)) ^ g.core
    shift = (spot // piece) % g.chips
    chip = ((g.x - shift // g.cols) % g.xs) * g.cols + (g.y - shift % g.cols) % g.cols
    inner = chip * piece + spot % piece
    patch = (core * half + inner % half) * SHUF + inner // half
    order = row_order(g)
    source = order[:, None] * group + jnp.arange(group, dtype=jnp.int32)[None, :]
    pick = (patch[:, None] == source.reshape(1, patches)).astype(BF)
    all_hidden = dot_nn(pick, all_hidden.reshape(patches, -1)).astype(BF)

    result = weight_grad(patch_grad, all_hidden, order, features, 1.0 / math.sqrt(patches))
    return result.T


def solution(mesh):
    placed = (
        P(None, ("enc", "col")),
        P("enc", "row"),
        P("enc", "row"),
        P(("enc", "col"), "row"),
        P(("enc", "col"), "row"),
        P("row", ("enc", "col")),
        P(None, ("enc", "col")),
        P("row", ("enc", "col")),
        P(),
        P(),
    )
    return jax.shard_map(
        shards, mesh=mesh, in_specs=placed, out_specs=P(None, ("enc", "col")), check_vma=False
    )
```

```python
import functools
import math

import jax
import jax.numpy as jnp
from jax import lax
from jax.experimental import pallas as pl
from jax.experimental.pallas import tpu as pltpu
from jax.sharding import PartitionSpec as P

SHUF = 4
CORES = 2
LANES = 128
AXES = ("enc", "row", "col")
BF = jnp.bfloat16
F32 = jnp.float32


def cdiv(a, b):
    return -(-a // b)


def dot_nt(left, right):
    return lax.dot_general(left, right, (((1,), (1,)), ((), ())), preferred_element_type=F32)


def dot_nn(left, right):
    return lax.dot_general(left, right, (((1,), (0,)), ((), ())), preferred_element_type=F32)


def dot_tn(left, right):
    return lax.dot_general(left, right, (((0,), (0,)), ((), ())), preferred_element_type=F32)


class Grid:
    def __init__(self):
        self.enc, self.rows, self.cols = (lax.axis_size(a) for a in AXES)
        self.xs = self.enc // CORES
        self.chips = self.xs * self.cols
        enc = lax.axis_index("enc")
        self.core = enc % CORES
        self.x = enc // CORES
        self.y = lax.axis_index("col")
        self.z = lax.axis_index("row")
        self.shifts = [(dx, dy) for dx in range(self.xs) for dy in range(self.cols)]

    def send(self, value, dx=0, dy=0, core=0, row=None):
        pairs = []
        for e in range(self.enc):
            for r in range(self.rows):
                for c in range(self.cols):
                    x, k = divmod(e, CORES)
                    target = (((x + dx) % self.xs) * CORES + (k ^ core), r if row is None else row(r), (c + dy) % self.cols)
                    flat = [(a * self.rows + b) * self.cols + d for a, b, d in ((e, r, c), target)]
                    pairs.append(tuple(flat))
        return lax.ppermute(value, AXES, pairs)

    def swap(self, value):
        return self.send(value, core=1)

    def place(self):
        return jnp.stack([self.core, self.x, self.y, self.z]).astype(jnp.int32)


MIB = 2**20
HINT = (4 * 10**10, 10**8)
VM = pl.BlockSpec(memory_space=pltpu.VMEM)
SM = pl.BlockSpec(memory_space=pltpu.SMEM)
HBM = pl.BlockSpec(memory_space=pltpu.HBM)


def local_call(kernel, name, out_shape, in_specs, args, limit, scratch=(), busy=(0, 0), out_specs=None):
    return pl.pallas_call(
        kernel,
        out_shape=out_shape,
        in_specs=in_specs,
        out_specs=jax.tree.map(lambda _: VM, out_shape) if out_specs is None else out_specs,
        scratch_shapes=list(scratch),
        compiler_params=pltpu.CompilerParams(vmem_limit_bytes=limit * MIB),
        cost_estimate=pl.CostEstimate(flops=busy[0], bytes_accessed=busy[1], transcendentals=0),
        name=name,
    )(*args)


def spans(total, step):
    return [(s, min(step, total - s)) for s in range(0, total, step)]


def down_matmul(g, at, out_grad, w_down, own, tall, share):
    slots, width = out_grad.shape
    units = w_down.shape[0]
    half = g.xs * tall
    parts = []
    for c in range(g.cols):
        valid = max(0, min(share, units - c * share))
        parts += [(c, off, n) for off, n in spans(valid, 2048)]

    def kernel(pos, grad_hbm, w_ref, keep_ref, give_ref, grad_ref, buf, sem):
        first = pltpu.make_async_copy(grad_hbm, grad_ref, sem.at[len(parts)])
        first.start()
        copies = []
        for i, (c, off, n) in enumerate(parts):
            span = pl.ds(c * share + off, n)
            copies.append(pltpu.make_async_copy(w_ref.at[span], buf.at[span], sem.at[i]))
            copies[-1].start()
        row = lax.broadcasted_iota(jnp.int32, (CORES * half, slots), 0)
        col = lax.broadcasted_iota(jnp.int32, (CORES * half, slots), 1)
        core, x, inner = row // half, row // tall % g.xs, row % tall
        device = (x + pos[1]) % g.xs * CORES + (core + pos[0]) % CORES
        pick = jnp.where((inner < own) & (col == device * own + inner), 1.0, 0.0).astype(BF)
        first.wait()
        left = dot_nn(pick, grad_ref[...]).astype(BF)
        for copy, (c, off, n) in zip(copies, parts):
            copy.wait()
            out = dot_nt(left, buf[c * share + off : c * share + off + n]).astype(BF)
            keep_ref[c, :, off : off + n] = out[:half]
            give_ref[c, :, off : off + n] = out[half:]
        for c in range(g.cols):
            valid = max(0, min(share, units - c * share))
            if valid < share:
                for ref in (keep_ref, give_ref):
                    ref[c, :, valid:] = jnp.zeros((half, share - valid), BF)

    shape = jax.ShapeDtypeStruct((g.cols, half, share), BF)
    return local_call(
        kernel, "down_matmul", [shape, shape], [SM, HBM, HBM], (at, out_grad, w_down), 52,
        [pltpu.VMEM((slots, width), BF), pltpu.VMEM((units, width), BF), pltpu.SemaphoreType.DMA((len(parts) + 1,))],
        busy=(2 * slots * units * width, 2 * units * width),
    )


def core_sum(g, at, keep, other, tall):
    share = keep.shape[2]

    def kernel(pos, keep_ref, other_ref, own_ref, *piece_refs):
        for (dx, dy), ref in zip(g.shifts, (own_ref,) + piece_refs):
            col = (pos[2] + dy) % g.cols
            rows = pl.ds(dx * tall, tall)
            ref[...] = (keep_ref[col, rows].astype(F32) + other_ref[col, rows].astype(F32)).astype(ref.dtype)

    shapes = [jax.ShapeDtypeStruct((tall, share), F32 if s == (0, 0) else BF) for s in g.shifts]
    return local_call(kernel, "core_sum", shapes, [SM, VM, VM], (at, keep, other), 4, busy=HINT)


def gate_grads(g, at, total, others, gate_pre, up_pre):
    share = total.shape[1]
    own, units = gate_pre.shape

    def kernel(pos, total_ref, *refs):
        other_refs, (gate_ref, up_ref, out_ref) = refs[:-3], refs[-3:]
        hidden = total_ref[...]
        for ref in other_refs:
            hidden = hidden + ref[...].astype(F32)
        hidden = hidden[:own]
        for c in range(g.cols):
            valid = max(0, min(share, units - c * share))

            @pl.when(pos[2] == c)
            def _():
                gate = gate_ref[:, c * share : c * share + valid].astype(F32)
                up = up_ref[:, c * share : c * share + valid].astype(F32)
                grad = hidden[:, :valid]
                squash = 1.0 / (1.0 + jnp.exp(-gate))
                base = grad * squash
                out_ref[:own, :valid] = (base * up * (1.0 + gate * (1.0 - squash))).astype(BF)
                out_ref[own:, :valid] = (base * gate).astype(BF)
                if valid < share:
                    out_ref[:, valid:] = jnp.zeros((2 * own, share - valid), BF)

    shape = jax.ShapeDtypeStruct((2 * own, share), BF)
    return local_call(
        kernel, "gate_grads", shape, [SM] + [VM] * (len(others) + 3),
        (at, total, *others, gate_pre, up_pre), 4, busy=HINT,
    )


def input_matmul(g, at, pieces, route, img_count, w_gate, w_up, own):
    share = pieces[0].shape[1]
    units, width = w_gate.shape
    slots = route.shape[1]
    image = slots // g.rows
    half = slots // CORES
    rows = len(pieces) // g.cols
    order = [(core, dx, dy) for core in range(CORES) for dx, dy in g.shifts]

    def kernel(pos, count_ref, *refs):
        piece_refs, (route_ref, gate_ref, up_ref, out_ref, left) = refs[: len(pieces)], refs[len(pieces) :]
        for (core, dx, dy), ref in zip(order, piece_refs):
            at_row = (core * g.xs + dx) * 2 * own
            left[(pos[2] - dy + g.cols) % g.cols, at_row : at_row + 2 * own] = ref[...]
        gate, up = 0.0, 0.0
        for c in range(g.cols):
            valid = max(0, min(share, units - c * share))
            for off, n in spans(valid, 1920):
                row = c * share + off
                part = left[c, :, off : off + n]
                gate = gate + dot_nn(part, gate_ref[row : row + n])
                up = up + dot_nn(part, up_ref[row : row + n])
        both = [gate[2 * r * own : 2 * r * own + own] + up[2 * r * own + own : 2 * (r + 1) * own] for r in range(rows)]
        line = route_ref[...]
        device, local = lax.div(line, own), lax.rem(line, own)
        x, core = lax.div(device, CORES), lax.rem(device, CORES)
        away = lax.rem(pos[1] - x + g.xs, g.xs)
        place = (lax.rem(core + pos[0], CORES) * g.xs + away) * own + local
        slot = lax.broadcasted_iota(jnp.int32, (1, slots), 1)
        live = jnp.zeros((1, slots), jnp.int32)
        for r in range(g.rows):
            live = jnp.where(lax.div(slot, image) == r, count_ref[r], live)
        place = jnp.where(lax.rem(slot, image) < live, place, -1)
        pick = jnp.where(lax.broadcasted_iota(jnp.int32, (slots, slots), 0) == place, 1.0, 0.0).astype(BF)
        done = dot_tn(pick, jnp.concatenate(both).astype(BF)).astype(BF)
        for k in range(CORES):

            @pl.when(pos[0] == k)
            def _():
                out_ref[:half] = done[k * half : (k + 1) * half]
                out_ref[half:] = done[(1 - k) * half : (2 - k) * half]

    return local_call(
        kernel, "input_matmul", jax.ShapeDtypeStruct((slots, width), BF), [SM, SM] + [VM] * (len(pieces) + 3),
        (at, img_count, *pieces, route, w_gate, w_up), 8,
        [pltpu.VMEM((g.cols, 2 * own * rows, share), BF)],
        busy=(8 * slots * units * width, 4 * units * width),
    )


def fetch_rows(g, at, w_proj, steps):
    block = SHUF * LANES
    last = cdiv(w_proj.shape[0], block) - 1

    def kernel(pos, w_ref, out_ref, sem):
        copies = []
        for i in range(steps):
            first = jnp.minimum(pos[3] * steps + i, last) * block
            copies.append(pltpu.make_async_copy(w_ref.at[pl.ds(first, block)], out_ref.at[i], sem.at[i]))
            copies[-1].start()
        for copy in copies:
            copy.wait()

    shape = jax.ShapeDtypeStruct((steps, block, w_proj.shape[1]), BF)
    return local_call(
        kernel, "fetch_rows", shape, [SM, HBM], (at, w_proj), 22, [pltpu.SemaphoreType.DMA((steps,))],
        busy=(0, 2 * steps * block * w_proj.shape[1]),
    )


def shuffle_matmul(g, image_grad, w_rows):
    slots, width = image_grad.shape
    half = slots // CORES
    steps, block, width = w_rows.shape
    sub = g.chips // SHUF
    piece = half // sub

    def kernel(grad_ref, w_ref, keep_ref, give_ref, parts):
        source = lax.broadcasted_iota(jnp.int32, (block, block), 0)
        target = lax.broadcasted_iota(jnp.int32, (block, block), 1)
        order = jnp.where(source == SHUF * (target % LANES) + target // LANES, 1.0, 0.0).astype(BF)
        for i in range(steps):
            parts[i * slots : (i + 1) * slots] = dot_nt(grad_ref[...], w_ref[i]).astype(BF)
        done = dot_nn(parts[...], order).astype(BF)
        for i in range(steps):
            for ref, top in ((keep_ref, i * slots), (give_ref, i * slots + half)):
                for q in range(SHUF):
                    for s in range(sub):
                        rows = done[top + s * piece : top + (s + 1) * piece, q * LANES : (q + 1) * LANES]
                        ref[q * sub + s, :, i * LANES : (i + 1) * LANES] = rows

    shape = jax.ShapeDtypeStruct((g.chips, piece, steps * LANES), BF)
    return local_call(
        kernel, "shuffle_matmul", [shape, shape], [VM, VM], (image_grad, w_rows), 8,
        [pltpu.VMEM((steps * slots, block), BF)],
        busy=(2 * slots * width * block * steps, 2 * width * block * steps),
    )


def chip_sum(g, at, keep, other):
    def kernel(pos, keep_ref, other_ref, own_ref, *piece_refs):
        for (dx, dy), ref in zip(g.shifts, (own_ref,) + piece_refs):
            chip = (pos[1] + dx) % g.xs * g.cols + (pos[2] + dy) % g.cols
            ref[...] = (keep_ref[chip].astype(F32) + other_ref[chip].astype(F32)).astype(ref.dtype)

    shapes = [jax.ShapeDtypeStruct(keep.shape[1:], F32 if s == (0, 0) else BF) for s in g.shifts]
    return local_call(kernel, "chip_sum", shapes, [SM, VM, VM], (at, keep, other), 4)


def order_hidden(g, at, parts, piece):
    group, units = parts[0].shape[1:]
    patches = group * g.rows
    half = patches // (CORES * SHUF)
    masks = row_masks(g)

    def kernel(pos, *refs):
        spot = lax.broadcasted_iota(jnp.int32, (patches, group), 0)
        inner = lax.rem(spot, piece)
        shift = lax.rem(lax.div(spot, piece), g.chips)
        core = lax.rem(lax.div(spot, g.chips * piece) + pos[0], CORES)
        x = lax.rem(pos[1] - lax.div(shift, g.cols) + g.xs, g.xs)
        y = lax.rem(pos[2] - lax.rem(shift, g.cols) + g.cols, g.cols)
        inner = (x * g.cols + y) * piece + inner
        patch = (core * half + lax.rem(inner, half)) * SHUF + lax.div(inner, half)
        source = lax.broadcasted_iota(jnp.int32, (patches, group), 1)
        total, i = 0.0, 0
        for ref in refs[:-1]:
            for part in range(ref.shape[0]):
                row = i if masks is None else masks[i] ^ pos[3]
                pick = jnp.where(patch == source + row * group, 1.0, 0.0).astype(BF)
                total = total + lax.dot_general(
                    ref[part], pick, (((0,), (1,)), ((), ())), preferred_element_type=F32
                )
                i += 1
        refs[-1][...] = total.astype(BF)

    shape = jax.ShapeDtypeStruct((units, patches), BF)
    return local_call(
        kernel, "order_hidden", shape, [SM] + [VM] * len(parts), (at, *parts), 8, busy=(2 * units * patches * patches, 0)
    )


def weight_grad(g, at, result, features, first, pieces, hidden):
    units, patches = hidden.shape
    count, piece, wide = pieces[0].shape
    scale = 1.0 / math.sqrt(patches)
    masks = row_masks(g)
    full, tail = divmod(features, wide)
    fresh = result is None

    def kernel(pos, *refs):
        refs = refs if fresh else refs[1:]
        piece_refs, (hidden_ref, out_ref, patch, buf, sem) = refs[:-5], refs[-5:]
        sends = []
        for i in range(count):
            row = first + i if masks is None else masks[first + i] ^ pos[3]
            for n, ref in enumerate(piece_refs):
                patch[i, n * piece : (n + 1) * piece] = ref[i]
            buf[i] = (dot_nn(hidden_ref[...], patch[i]) * scale).astype(BF)
            begun = []
            if masks is not None or row < full:
                ends = out_ref.at[:, pl.ds(row * wide, wide)]
                begun.append((row < full, pltpu.make_async_copy(buf.at[i], ends, sem.at[i])))
            if tail:
                ends = out_ref.at[:, pl.ds(full * wide, tail)]
                begun.append((row == full, pltpu.make_async_copy(buf.at[i, :, pl.ds(0, tail)], ends, sem.at[i])))
            for now, copy in begun:
                pl.when(now)(copy.start)
            sends += begun
        for now, copy in sends:
            pl.when(now)(copy.wait)

    return pl.pallas_call(
        kernel,
        out_shape=jax.ShapeDtypeStruct((units, features), BF),
        in_specs=[SM] + ([] if fresh else [HBM]) + [VM] * (len(pieces) + 1),
        out_specs=HBM,
        scratch_shapes=[
            pltpu.VMEM((count, patches, wide), BF),
            pltpu.VMEM((count, units, wide), BF),
            pltpu.SemaphoreType.DMA((count,)),
        ],
        input_output_aliases={} if fresh else {1: 0},
        compiler_params=pltpu.CompilerParams(vmem_limit_bytes=16 * MIB),
        cost_estimate=pl.CostEstimate(
            flops=2 * count * patches * wide * units, bytes_accessed=2 * count * units * wide, transcendentals=0
        ),
        name="weight_grad",
    )(at, *([] if fresh else [result]), *pieces, hidden)


def row_masks(g):
    if g.rows & (g.rows - 1):
        return None
    masks = [0]
    while len(masks) < g.rows:
        masks = masks + [m ^ (2 * len(masks) - 1) for m in masks]
    return masks


def sum_rows(g, value, beside):
    if g.rows & (g.rows - 1):
        return lax.psum(value.astype(F32), "row").astype(BF), beside
    beside, step, n = list(beside), 1, 0
    while step < g.rows:
        mask = 2 * step - 1
        other = g.send(value, row=lambda r: r ^ mask)
        if n < len(beside):
            other, beside[n] = lax.optimization_barrier((other, beside[n]))
        value = (value.astype(F32) + other.astype(F32)).astype(BF)
        step, n = 2 * step, n + 1
    return value, beside


def ordered(first, *later):
    return lax.optimization_barrier((first, *later))[1:]


def shards(out_grad, gate_pre, up_pre, w_gate, w_up, w_down, w_proj, enc_hidden, route, img_count):
    g = Grid()
    at = g.place()
    slots = route.shape[0]
    own = gate_pre.shape[0]
    half = slots // CORES
    units = w_down.shape[0]
    tall = cdiv(own, 16) * 16
    share = cdiv(cdiv(units, g.cols), LANES) * LANES
    doubling = not g.rows & (g.rows - 1)

    def to_chips(pieces):
        return [g.send(p, dx=dx, dy=dy) for p, (dx, dy) in zip(pieces, g.shifts[1:])]

    saved = enc_hidden[None]
    keep, give = down_matmul(g, at, out_grad, w_down, own, tall, share)
    total, *pieces = core_sum(g, at, keep, g.swap(give), tall)
    saved_parts = [saved]
    if doubling and g.rows > 1:
        (mine,) = ordered(total, saved)
        saved_parts.append(g.send(mine, row=lambda r: r ^ 1))
        total, *pieces = lax.optimization_barrier((total, *pieces))
    arrived = to_chips(pieces)
    if doubling and g.rows > 1:
        saved_parts[1], *arrived = lax.optimization_barrier((saved_parts[1], *arrived))
    grads = gate_grads(g, at, total, arrived, gate_pre, up_pre)
    step = 2
    while doubling and step < g.rows:
        (mine,) = ordered(grads, jnp.concatenate(saved_parts))
        mask = 2 * step - 1
        saved_parts.append(g.send(mine, row=lambda r: r ^ mask))
        step *= 2
    pieces = [grads] + to_chips([grads] * (g.chips - 1))
    pieces = pieces + [g.swap(p) for p in pieces]
    if not doubling:
        saved_parts = [lax.all_gather(enc_hidden, "row", axis=0, tiled=False)]
    image_grad = input_matmul(g, at, pieces, route.reshape(1, slots), img_count, w_gate.T, w_up.T, own)

    features = w_proj.shape[0] // SHUF
    steps = cdiv(cdiv(features, g.rows), LANES)
    piece = SHUF * half // g.chips
    image_grad, late = lax.optimization_barrier((image_grad, at))
    w_rows = fetch_rows(g, late, w_proj, steps)
    hidden = order_hidden(g, late, saved_parts, piece)
    image_grad, (hidden, w_rows) = sum_rows(g, image_grad, (hidden, w_rows))

    keep, give = shuffle_matmul(g, image_grad, w_rows)
    total, *pieces = chip_sum(g, at, keep, g.swap(give))
    for part in to_chips(pieces):
        total = total + part.astype(F32)
    patch_grad = total.astype(BF)

    if not doubling:
        batches = [lax.all_gather(patch_grad, "row", axis=0, tiled=False)]
    else:
        stack, batches, step = patch_grad[None], [], 1
        while step < g.rows:
            mask = 2 * step - 1
            other = g.send(stack, row=lambda r: r ^ mask)
            stack = jnp.concatenate([stack, other])
            batches.append(stack if step == 1 else other)
            step *= 2
        batches = batches or [stack]
    result, first = None, 0
    for batch in batches:
        pieces = [batch] + to_chips([batch] * (g.chips - 1))
        pieces = pieces + [g.swap(p) for p in pieces]
        result = weight_grad(g, at, result, features, first, pieces, hidden)
        first += batch.shape[0]
    return result.T


def solution(mesh):
    placed = (
        P(None, ("enc", "col")),
        P("enc", "row"),
        P("enc", "row"),
        P(("enc", "col"), "row"),
        P(("enc", "col"), "row"),
        P("row", ("enc", "col")),
        P(None, ("enc", "col")),
        P("row", ("enc", "col")),
        P(),
        P(),
    )
    return jax.shard_map(
        shards, mesh=mesh, in_specs=placed, out_specs=P(None, ("enc", "col")), check_vma=False
    )
```

```python
import math

import jax
import jax.numpy as jnp
from jax import lax
from jax.experimental import pallas as pl
from jax.experimental.pallas import tpu as pltpu
from jax.sharding import PartitionSpec as P

SHUF = 4
CORES = 2
LANES = 128
AXES = ("enc", "row", "col")
BF = jnp.bfloat16
F32 = jnp.float32


def cdiv(a, b):
    return -(-a // b)


def dot_nt(left, right):
    return lax.dot_general(left, right, (((1,), (1,)), ((), ())), preferred_element_type=F32)


def dot_nn(left, right):
    return lax.dot_general(left, right, (((1,), (0,)), ((), ())), preferred_element_type=F32)


def dot_tn(left, right):
    return lax.dot_general(left, right, (((0,), (0,)), ((), ())), preferred_element_type=F32)


class Grid:
    def __init__(self):
        self.enc, self.rows, self.cols = (lax.axis_size(a) for a in AXES)
        self.xs = self.enc // CORES
        self.chips = self.xs * self.cols
        enc = lax.axis_index("enc")
        self.core = enc % CORES
        self.x = enc // CORES
        self.y = lax.axis_index("col")
        self.z = lax.axis_index("row")
        self.shifts = [(dx, dy) for dx in range(self.xs) for dy in range(self.cols)]

    def send(self, value, dx=0, dy=0, core=0, row=None):
        pairs = []
        for e in range(self.enc):
            for r in range(self.rows):
                for c in range(self.cols):
                    x, k = divmod(e, CORES)
                    target = (((x + dx) % self.xs) * CORES + (k ^ core), r if row is None else row(r), (c + dy) % self.cols)
                    flat = [(a * self.rows + b) * self.cols + d for a, b, d in ((e, r, c), target)]
                    pairs.append(tuple(flat))
        return lax.ppermute(value, AXES, pairs)

    def swap(self, value):
        return self.send(value, core=1)

    def place(self):
        return jnp.stack([self.core, self.x, self.y, self.z]).astype(jnp.int32)


MIB = 2**20
HINT = (4 * 10**10, 10**8)
VM = pl.BlockSpec(memory_space=pltpu.VMEM)
SM = pl.BlockSpec(memory_space=pltpu.SMEM)
HBM = pl.BlockSpec(memory_space=pltpu.HBM)


def local_call(kernel, out_shape, in_specs, args, limit, scratch=(), busy=(0, 0), out_specs=None):
    return pl.pallas_call(
        kernel,
        out_shape=out_shape,
        in_specs=in_specs,
        out_specs=jax.tree.map(lambda _: VM, out_shape) if out_specs is None else out_specs,
        scratch_shapes=list(scratch),
        compiler_params=pltpu.CompilerParams(vmem_limit_bytes=limit * MIB),
        cost_estimate=pl.CostEstimate(flops=busy[0], bytes_accessed=busy[1], transcendentals=0),
    )(*args)


def in_hbm(value):
    return pltpu.with_memory_space_constraint(value, pltpu.HBM)


def spans(total, step):
    return [(s, min(step, total - s)) for s in range(0, total, step)]


def down_matmul(g, at, out_grad, w_down, own, tall, share):
    slots, width = out_grad.shape
    units = w_down.shape[0]
    half = g.xs * tall
    parts = []
    for c in range(g.cols):
        valid = max(0, min(share, units - c * share))
        parts += [(c, off, n) for off, n in spans(valid, 2048)]

    def kernel(pos, grad_hbm, w_ref, keep_ref, give_ref, grad_ref, buf, sem):
        first = pltpu.make_async_copy(grad_hbm, grad_ref, sem.at[len(parts)])
        first.start()
        copies = []
        for i, (c, off, n) in enumerate(parts):
            span = pl.ds(c * share + off, n)
            copies.append(pltpu.make_async_copy(w_ref.at[span], buf.at[span], sem.at[i]))
            copies[-1].start()
        row = lax.broadcasted_iota(jnp.int32, (CORES * half, slots), 0)
        col = lax.broadcasted_iota(jnp.int32, (CORES * half, slots), 1)
        core, x, inner = row // half, row // tall % g.xs, row % tall
        device = (x + pos[1]) % g.xs * CORES + (core + pos[0]) % CORES
        pick = jnp.where((inner < own) & (col == device * own + inner), 1.0, 0.0).astype(BF)
        first.wait()
        left = dot_nn(pick, grad_ref[...]).astype(BF)
        for copy, (c, off, n) in zip(copies, parts):
            copy.wait()
            out = dot_nt(left, buf[c * share + off : c * share + off + n]).astype(BF)
            keep_ref[c, :, off : off + n] = out[:half]
            give_ref[c, :, off : off + n] = out[half:]
        for c in range(g.cols):
            valid = max(0, min(share, units - c * share))
            if valid < share:
                for ref in (keep_ref, give_ref):
                    ref[c, :, valid:] = jnp.zeros((half, share - valid), BF)

    shape = jax.ShapeDtypeStruct((g.cols, half, share), BF)
    return local_call(
        kernel, [shape, shape], [SM, HBM, HBM], (at, in_hbm(out_grad), in_hbm(w_down)), 52,
        [pltpu.VMEM((slots, width), BF), pltpu.VMEM((units, width), BF), pltpu.SemaphoreType.DMA((len(parts) + 1,))],
        busy=(2 * slots * units * width, 2 * units * width),
    )


def core_sum(g, at, keep, other, tall):
    share = keep.shape[2]
    fold = cdiv(share // LANES, 2) * LANES

    def kernel(pos, keep_ref, other_ref, own_ref, *piece_refs):
        for (dx, dy), ref in zip(g.shifts, (own_ref,) + piece_refs):
            col = (pos[2] + dy) % g.cols
            both = keep_ref[col].astype(F32) + other_ref[col].astype(F32)
            part = both[dx * tall : (dx + 1) * tall]
            if (dx, dy) == (0, 0):
                ref[...] = part
            else:
                ref[:tall] = part[:, :fold].astype(BF)
                ref[tall:, : share - fold] = part[:, fold:].astype(BF)
                if share < 2 * fold:
                    ref[tall:, share - fold :] = jnp.zeros((tall, 2 * fold - share), BF)

    shapes = [
        jax.ShapeDtypeStruct((tall, share), F32) if s == (0, 0) else jax.ShapeDtypeStruct((2 * tall, fold), BF)
        for s in g.shifts
    ]
    return local_call(kernel, shapes, [SM, VM, VM], (at, keep, other), 4, busy=HINT)


def gate_grads(g, at, total, others, gate_pre, up_pre):
    own, units = gate_pre.shape
    share = total.shape[1]
    fold = cdiv(share // LANES, 2) * LANES

    def kernel(pos, total_ref, *refs):
        other_refs, (gate_ref, up_ref, out_ref) = refs[:-3], refs[-3:]
        for low, high in ((0, fold), (fold, share)):
            grad = total_ref[:, low:high]
            for ref in other_refs:
                folded = ref[...].astype(F32)
                grad = grad + (folded[:own] if low == 0 else folded[own:, : high - low])
            for c in range(g.cols):
                valid = max(0, min(high, units - c * share) - low)

                @pl.when(pos[2] == c)
                def _():
                    if valid:
                        start = c * share + low
                        gate = gate_ref[:, start : start + valid].astype(F32)
                        up = up_ref[:, start : start + valid].astype(F32)
                        squash = 1.0 / (1.0 + jnp.exp(-gate))
                        base = grad[:, :valid] * squash
                        out_ref[:own, low : low + valid] = (base * up * (1.0 + gate * (1.0 - squash))).astype(BF)
                        out_ref[own:, low : low + valid] = (base * gate).astype(BF)
                    if valid < high - low:
                        out_ref[:, low + valid : high] = jnp.zeros((2 * own, high - low - valid), BF)

    shape = jax.ShapeDtypeStruct((2 * own, share), BF)
    return local_call(
        kernel, shape, [SM] + [VM] * (len(others) + 3),
        (at, total, *others, gate_pre, up_pre), 6, busy=HINT,
    )


def input_matmul(g, at, pieces, route, img_count, w_gate, w_up, own):
    share = pieces[0].shape[1]
    units, width = w_gate.shape
    slots = route.shape[1]
    image = slots // g.rows
    half = slots // CORES
    rows = len(pieces) // g.cols
    order = [(core, dx, dy) for core in range(CORES) for dx, dy in g.shifts]

    def kernel(pos, count_ref, *refs):
        piece_refs, (route_ref, gate_ref, up_ref, out_ref, left) = refs[: len(pieces)], refs[len(pieces) :]
        for (core, dx, dy), ref in zip(order, piece_refs):
            at_row = (core * g.xs + dx) * 2 * own
            left[(pos[2] - dy + g.cols) % g.cols, at_row : at_row + 2 * own] = ref[...]
        gate, up = 0.0, 0.0
        for c in range(g.cols):
            valid = max(0, min(share, units - c * share))
            for off, n in spans(valid, 1920):
                row = c * share + off
                part = left[c, :, off : off + n]
                gate = gate + dot_nn(part, gate_ref[row : row + n])
                up = up + dot_nn(part, up_ref[row : row + n])
        both = [gate[2 * r * own : 2 * r * own + own] + up[2 * r * own + own : 2 * (r + 1) * own] for r in range(rows)]
        line = route_ref[...]
        device, local = lax.div(line, own), lax.rem(line, own)
        x, core = lax.div(device, CORES), lax.rem(device, CORES)
        away = lax.rem(pos[1] - x + g.xs, g.xs)
        place = (lax.rem(core + pos[0], CORES) * g.xs + away) * own + local
        slot = lax.broadcasted_iota(jnp.int32, (1, slots), 1)
        live = jnp.zeros((1, slots), jnp.int32)
        for r in range(g.rows):
            live = jnp.where(lax.div(slot, image) == r, count_ref[r], live)
        place = jnp.where(lax.rem(slot, image) < live, place, -1)
        pick = jnp.where(lax.broadcasted_iota(jnp.int32, (slots, slots), 0) == place, 1.0, 0.0).astype(BF)
        done = dot_tn(pick, jnp.concatenate(both).astype(BF)).astype(BF)
        for k in range(CORES):

            @pl.when(pos[0] == k)
            def _():
                out_ref[:half] = done[k * half : (k + 1) * half]
                out_ref[half:] = done[(1 - k) * half : (2 - k) * half]

    return local_call(
        kernel, jax.ShapeDtypeStruct((slots, width), BF), [SM, SM] + [VM] * (len(pieces) + 3),
        (at, img_count, *pieces, route, w_gate, w_up), 8,
        [pltpu.VMEM((g.cols, 2 * own * rows, share), BF)],
        busy=(8 * slots * units * width, 4 * units * width),
    )


def fetch_rows(at, w_proj, steps, start, count):
    block = SHUF * LANES
    last = cdiv(w_proj.shape[0], block) - 1

    def kernel(pos, w_ref, out_ref, sem):
        copies = []
        for i in range(count):
            first = jnp.minimum(pos[3] * steps + start + i, last) * block
            copies.append(pltpu.make_async_copy(w_ref.at[pl.ds(first, block)], out_ref.at[i], sem.at[i]))
            copies[-1].start()
        for copy in copies:
            copy.wait()

    shape = jax.ShapeDtypeStruct((count, block, w_proj.shape[1]), BF)
    return local_call(
        kernel, shape, [SM, HBM], (at, in_hbm(w_proj)), 22, [pltpu.SemaphoreType.DMA((count,))],
        busy=(0, 2 * count * block * w_proj.shape[1]),
    )


def shuffle_matmul(g, image_grad, w_parts):
    slots, width = image_grad.shape
    half = slots // CORES
    block, width = w_parts[0].shape[1:]
    steps = sum(w.shape[0] for w in w_parts)
    sub = g.chips // SHUF
    piece = half // sub

    def kernel(grad_ref, *refs):
        w_refs, (keep_ref, give_ref, parts) = refs[: len(w_parts)], refs[len(w_parts) :]
        blocks = [(ref, n) for ref in w_refs for n in range(ref.shape[0])]
        source = lax.broadcasted_iota(jnp.int32, (block, block), 0)
        target = lax.broadcasted_iota(jnp.int32, (block, block), 1)
        order = jnp.where(source == SHUF * (target % LANES) + target // LANES, 1.0, 0.0).astype(BF)
        for i, (ref, n) in enumerate(blocks):
            parts[i * slots : (i + 1) * slots] = dot_nt(grad_ref[...], ref[n]).astype(BF)
        done = dot_nn(parts[...], order).astype(BF)
        for i in range(steps):
            for ref, top in ((keep_ref, i * slots), (give_ref, i * slots + half)):
                for q in range(SHUF):
                    for s in range(sub):
                        rows = done[top + s * piece : top + (s + 1) * piece, q * LANES : (q + 1) * LANES]
                        ref[q * sub + s, :, i * LANES : (i + 1) * LANES] = rows

    shape = jax.ShapeDtypeStruct((g.chips, piece, steps * LANES), BF)
    return local_call(
        kernel, [shape, shape], [VM] * (1 + len(w_parts)), (image_grad, *w_parts), 8,
        [pltpu.VMEM((steps * slots, block), BF)],
        busy=(2 * slots * width * block * steps, 2 * width * block * steps),
    )


def chip_sum(g, at, keep, other):
    def kernel(pos, keep_ref, other_ref, own_ref, *piece_refs):
        for (dx, dy), ref in zip(g.shifts, (own_ref,) + piece_refs):
            chip = (pos[1] + dx) % g.xs * g.cols + (pos[2] + dy) % g.cols
            ref[...] = (keep_ref[chip].astype(F32) + other_ref[chip].astype(F32)).astype(ref.dtype)

    shapes = [jax.ShapeDtypeStruct(keep.shape[1:], F32 if s == (0, 0) else BF) for s in g.shifts]
    return local_call(kernel, shapes, [SM, VM, VM], (at, keep, other), 4)


def order_hidden(g, at, parts, piece):
    group, units = parts[0].shape[1:]
    patches = group * g.rows
    half = patches // (CORES * SHUF)
    masks = row_masks(g)

    def kernel(pos, *refs):
        spot = lax.broadcasted_iota(jnp.int32, (patches, group), 0)
        inner = lax.rem(spot, piece)
        shift = lax.rem(lax.div(spot, piece), g.chips)
        core = lax.rem(lax.div(spot, g.chips * piece) + pos[0], CORES)
        x = lax.rem(pos[1] - lax.div(shift, g.cols) + g.xs, g.xs)
        y = lax.rem(pos[2] - lax.rem(shift, g.cols) + g.cols, g.cols)
        inner = (x * g.cols + y) * piece + inner
        patch = (core * half + lax.rem(inner, half)) * SHUF + lax.div(inner, half)
        source = lax.broadcasted_iota(jnp.int32, (patches, group), 1)
        total, i = 0.0, 0
        for ref in refs[:-1]:
            for part in range(ref.shape[0]):
                row = i if masks is None else masks[i] ^ pos[3]
                pick = jnp.where(patch == source + row * group, 1.0, 0.0).astype(BF)
                total = total + lax.dot_general(
                    ref[part], pick, (((0,), (1,)), ((), ())), preferred_element_type=F32
                )
                i += 1
        refs[-1][...] = total.astype(BF)

    shape = jax.ShapeDtypeStruct((units, patches), BF)
    return local_call(kernel, shape, [SM] + [VM] * len(parts), (at, *parts), 8, busy=(2 * units * patches * patches, 0))


def weight_grad(g, at, result, features, first, pieces, hidden):
    units, patches = hidden.shape
    count, piece, wide = pieces[0].shape
    scale = 1.0 / math.sqrt(patches)
    masks = row_masks(g)
    full, tail = divmod(features, wide)
    parts = spans(wide, 2 * cdiv(wide, 4 * LANES) * LANES)
    fresh = result is None

    def kernel(pos, *refs):
        refs = refs if fresh else refs[1:]
        piece_refs, (hidden_ref, out_ref, patch, buf, sem) = refs[:-5], refs[-5:]
        sends = []
        for i in range(count):
            row = first + i if masks is None else masks[first + i] ^ pos[3]
            for n, ref in enumerate(piece_refs):
                patch[i, n * piece : (n + 1) * piece] = ref[i]
            for n, (off, size) in enumerate(parts):
                buf[i, :, off : off + size] = (dot_nn(hidden_ref[...], patch[i, :, off : off + size]) * scale).astype(BF)
                done = sem.at[i * len(parts) + n]
                begun = []
                if masks is not None or row < full:
                    ends = out_ref.at[:, pl.ds(row * wide + off, size)]
                    begun.append((row < full, pltpu.make_async_copy(buf.at[i, :, pl.ds(off, size)], ends, done)))
                rest = min(size, tail - off)
                if rest > 0:
                    ends = out_ref.at[:, pl.ds(full * wide + off, rest)]
                    begun.append((row == full, pltpu.make_async_copy(buf.at[i, :, pl.ds(off, rest)], ends, done)))
                for now, copy in begun:
                    pl.when(now)(copy.start)
                sends += begun
        for now, copy in sends:
            pl.when(now)(copy.wait)

    return pl.pallas_call(
        kernel,
        out_shape=jax.ShapeDtypeStruct((units, features), BF),
        in_specs=[SM] + ([] if fresh else [HBM]) + [VM] * (len(pieces) + 1),
        out_specs=HBM,
        scratch_shapes=[
            pltpu.VMEM((count, patches, wide), BF),
            pltpu.VMEM((count, units, wide), BF),
            pltpu.SemaphoreType.DMA((count * len(parts),)),
        ],
        input_output_aliases={} if fresh else {1: 0},
        compiler_params=pltpu.CompilerParams(vmem_limit_bytes=16 * MIB),
        cost_estimate=pl.CostEstimate(
            flops=2 * count * patches * wide * units, bytes_accessed=2 * count * units * wide, transcendentals=0
        ),
        name="weight_grad",
    )(at, *([] if fresh else [result]), *pieces, hidden)


def row_masks(g):
    if g.rows & (g.rows - 1):
        return None
    masks = [0]
    while len(masks) < g.rows:
        masks = masks + [m ^ (2 * len(masks) - 1) for m in masks]
    return masks


def sum_rows(g, value, beside):
    if g.rows & (g.rows - 1):
        return lax.psum(value.astype(F32), "row").astype(BF), beside
    beside, step, n = list(beside), 1, 0
    while step < g.rows:
        mask = 2 * step - 1
        other = g.send(value, row=lambda r: r ^ mask)
        if n < len(beside):
            other, beside[n] = lax.optimization_barrier((other, beside[n]))
        value = (value.astype(F32) + other.astype(F32)).astype(BF)
        step, n = 2 * step, n + 1
    return value, beside


def ordered(first, *later):
    return lax.optimization_barrier((first, *later))[1:]


def image_block(out_grad, gate_pre, up_pre, w_gate, w_up, w_down, w_proj, enc_hidden, route, img_count):
    g = Grid()
    at = g.place()
    slots = route.shape[0]
    own = gate_pre.shape[0]
    half = slots // CORES
    units = w_down.shape[0]
    tall = own
    share = cdiv(cdiv(units, g.cols), LANES) * LANES
    doubling = not g.rows & (g.rows - 1)

    def to_chips(pieces):
        return [g.send(p, dx=dx, dy=dy) for p, (dx, dy) in zip(pieces, g.shifts[1:])]

    saved = enc_hidden[None]
    keep, give = down_matmul(g, at, out_grad, w_down, own, tall, share)
    total, *pieces = core_sum(g, at, keep, g.swap(give), tall)
    saved_parts = [saved]
    if doubling and g.rows > 1:
        (mine,) = ordered(total, saved)
        saved_parts.append(g.send(mine, row=lambda r: r ^ 1))
        total, *pieces = lax.optimization_barrier((total, *pieces))
    arrived = to_chips(pieces)
    if doubling and g.rows > 1:
        saved_parts[1], *arrived = lax.optimization_barrier((saved_parts[1], *arrived))
    grads = gate_grads(g, at, total, arrived, gate_pre, up_pre)
    step = 2
    while doubling and step < g.rows:
        (mine,) = ordered(grads, jnp.concatenate(saved_parts))
        mask = 2 * step - 1
        saved_parts.append(g.send(mine, row=lambda r: r ^ mask))
        step *= 2
    pieces = [grads] + to_chips([grads] * (g.chips - 1))
    swapped = [g.swap(grads)]
    pieces = pieces + swapped + [g.swap(p) for p in pieces[1:]]
    if not doubling:
        saved_parts = [lax.all_gather(enc_hidden, "row", axis=0, tiled=False)]
    image_grad = input_matmul(g, at, pieces, route.reshape(1, slots), img_count, w_gate.T, w_up.T, own)

    features = w_proj.shape[0] // SHUF
    steps = cdiv(cdiv(features, g.rows), LANES)
    piece = SHUF * half // g.chips
    image_grad, late = lax.optimization_barrier((image_grad, at))
    early = steps // 2 + 1
    w_parts = [fetch_rows(late, w_proj, steps, s, n) for s, n in ((0, early), (early, steps - early)) if n]
    image_grad, w_parts = sum_rows(g, image_grad, w_parts)

    keep, give = shuffle_matmul(g, image_grad, w_parts)
    total, *pieces = chip_sum(g, at, keep, g.swap(give))
    for part in to_chips(pieces):
        total = total + part.astype(F32)
    patch_grad = total.astype(BF)
    late, patch_grad = lax.optimization_barrier((at, patch_grad))
    hidden = order_hidden(g, late, saved_parts, piece)

    if not doubling:
        batches = [lax.all_gather(patch_grad, "row", axis=0, tiled=False)]
    else:
        stack, batches, step = patch_grad[None], [], 1
        while step < g.rows:
            mask = 2 * step - 1
            other = g.send(stack, row=lambda r: r ^ mask)
            if step == 1:
                other, hidden = lax.optimization_barrier((other, hidden))
            stack = jnp.concatenate([stack, other])
            batches.append(stack if step == 1 else other)
            step *= 2
        batches = batches or [stack]
    result, first = None, 0
    held = []
    for batch in batches:
        held.append([batch] + to_chips([batch] * (g.chips - 1)))
    for batch, pieces in zip(batches, held):
        if result is not None:
            result, *pieces = lax.optimization_barrier((result, *pieces))
        others = [g.swap(batch)]
        others += [g.swap(p) for p in pieces[1:]]
        result = weight_grad(g, at, result, features, first, pieces + others, hidden)
        first += batch.shape[0]
    return result.T


def solution(mesh):
    placed = (
        P(None, ("enc", "col")),
        P("enc", "row"),
        P("enc", "row"),
        P(("enc", "col"), "row"),
        P(("enc", "col"), "row"),
        P("row", ("enc", "col")),
        P(None, ("enc", "col")),
        P("row", ("enc", "col")),
        P(),
        P(),
    )
    return jax.shard_map(image_block, mesh=mesh, in_specs=placed, out_specs=P(None, ("enc", "col")), check_vma=False)
```

```python
import math

import jax
import jax.numpy as jnp
from jax import lax
from jax.experimental import pallas as pl
from jax.experimental.pallas import tpu as pltpu
from jax.sharding import PartitionSpec as P

SHUF = 4
CORES = 2
LANES = 128
AXES = ("enc", "row", "col")
BF = jnp.bfloat16
F32 = jnp.float32


def cdiv(a, b):
    return -(-a // b)


def dot_nt(left, right):
    return lax.dot_general(left, right, (((1,), (1,)), ((), ())), preferred_element_type=F32)


def dot_nn(left, right):
    return lax.dot_general(left, right, (((1,), (0,)), ((), ())), preferred_element_type=F32)


def dot_tn(left, right):
    return lax.dot_general(left, right, (((0,), (0,)), ((), ())), preferred_element_type=F32)


class Grid:
    def __init__(self):
        self.enc, self.rows, self.cols = (lax.axis_size(a) for a in AXES)
        self.xs = self.enc // CORES
        self.chips = self.xs * self.cols
        enc = lax.axis_index("enc")
        self.core = enc % CORES
        self.x = enc // CORES
        self.y = lax.axis_index("col")
        self.z = lax.axis_index("row")
        self.shifts = [(dx, dy) for dx in range(self.xs) for dy in range(self.cols)]

    def send(self, value, dx=0, dy=0, core=0, row=None):
        pairs = []
        for e in range(self.enc):
            for r in range(self.rows):
                for c in range(self.cols):
                    x, k = divmod(e, CORES)
                    target = (((x + dx) % self.xs) * CORES + (k ^ core), r if row is None else row(r), (c + dy) % self.cols)
                    flat = [(a * self.rows + b) * self.cols + d for a, b, d in ((e, r, c), target)]
                    pairs.append(tuple(flat))
        return lax.ppermute(value, AXES, pairs)

    def swap(self, value):
        return self.send(value, core=1)

    def place(self):
        return jnp.stack([self.core, self.x, self.y, self.z]).astype(jnp.int32)


MIB = 2**20
HINT = (4 * 10**10, 10**8)
VM = pl.BlockSpec(memory_space=pltpu.VMEM)
SM = pl.BlockSpec(memory_space=pltpu.SMEM)
HBM = pl.BlockSpec(memory_space=pltpu.HBM)


def local_call(kernel, out_shape, in_specs, args, limit, scratch=(), busy=(0, 0), out_specs=None):
    return pl.pallas_call(
        kernel,
        out_shape=out_shape,
        in_specs=in_specs,
        out_specs=jax.tree.map(lambda _: VM, out_shape) if out_specs is None else out_specs,
        scratch_shapes=list(scratch),
        compiler_params=pltpu.CompilerParams(vmem_limit_bytes=limit * MIB),
        cost_estimate=pl.CostEstimate(flops=busy[0], bytes_accessed=busy[1], transcendentals=0),
    )(*args)


def in_hbm(value):
    return pltpu.with_memory_space_constraint(value, pltpu.HBM)


def spans(total, step):
    return [(s, min(step, total - s)) for s in range(0, total, step)]


def down_matmul(g, at, out_grad, w_down, own, tall, share):
    slots, width = out_grad.shape
    units = w_down.shape[0]
    half = g.xs * tall
    parts = []
    for c in range(g.cols):
        valid = max(0, min(share, units - c * share))
        parts += [(c, off, n) for off, n in spans(valid, 2048)]

    def kernel(pos, grad_hbm, w_ref, keep_ref, give_ref, grad_ref, buf, sem):
        first = pltpu.make_async_copy(grad_hbm, grad_ref, sem.at[len(parts)])
        first.start()
        copies = []
        for i, (c, off, n) in enumerate(parts):
            span = pl.ds(c * share + off, n)
            copies.append(pltpu.make_async_copy(w_ref.at[span], buf.at[span], sem.at[i]))
            copies[-1].start()
        row = lax.broadcasted_iota(jnp.int32, (CORES * half, slots), 0)
        col = lax.broadcasted_iota(jnp.int32, (CORES * half, slots), 1)
        core, x, inner = row // half, row // tall % g.xs, row % tall
        device = (x + pos[1]) % g.xs * CORES + (core + pos[0]) % CORES
        pick = jnp.where((inner < own) & (col == device * own + inner), 1.0, 0.0).astype(BF)
        first.wait()
        left = dot_nn(pick, grad_ref[...]).astype(BF)
        for copy, (c, off, n) in zip(copies, parts):
            copy.wait()
            out = dot_nt(left, buf[c * share + off : c * share + off + n]).astype(BF)
            keep_ref[c, :, off : off + n] = out[:half]
            give_ref[c, :, off : off + n] = out[half:]
        for c in range(g.cols):
            valid = max(0, min(share, units - c * share))
            if valid < share:
                for ref in (keep_ref, give_ref):
                    ref[c, :, valid:] = jnp.zeros((half, share - valid), BF)

    shape = jax.ShapeDtypeStruct((g.cols, half, share), BF)
    return local_call(
        kernel, [shape, shape], [SM, HBM, HBM], (at, in_hbm(out_grad), in_hbm(w_down)), 52,
        [pltpu.VMEM((slots, width), BF), pltpu.VMEM((units, width), BF), pltpu.SemaphoreType.DMA((len(parts) + 1,))],
        busy=(2 * slots * units * width, 2 * units * width),
    )


def core_sum(g, at, keep, other, tall):
    share = keep.shape[2]
    fold = cdiv(share // LANES, 2) * LANES

    def kernel(pos, keep_ref, other_ref, own_ref, *piece_refs):
        for (dx, dy), ref in zip(g.shifts, (own_ref,) + piece_refs):
            col = (pos[2] + dy) % g.cols
            both = keep_ref[col].astype(F32) + other_ref[col].astype(F32)
            part = both[dx * tall : (dx + 1) * tall]
            if (dx, dy) == (0, 0):
                ref[...] = part
            else:
                ref[:tall] = part[:, :fold].astype(BF)
                ref[tall:, : share - fold] = part[:, fold:].astype(BF)
                if share < 2 * fold:
                    ref[tall:, share - fold :] = jnp.zeros((tall, 2 * fold - share), BF)

    shapes = [
        jax.ShapeDtypeStruct((tall, share), F32) if s == (0, 0) else jax.ShapeDtypeStruct((2 * tall, fold), BF)
        for s in g.shifts
    ]
    return local_call(kernel, shapes, [SM, VM, VM], (at, keep, other), 4, busy=HINT)


def gate_grads(g, at, total, others, gate_pre, up_pre):
    own, units = gate_pre.shape
    share = total.shape[1]
    fold = cdiv(share // LANES, 2) * LANES

    def kernel(pos, total_ref, *refs):
        other_refs, (gate_ref, up_ref, out_ref) = refs[:-3], refs[-3:]
        for low, high in ((0, fold), (fold, share)):
            grad = total_ref[:, low:high]
            for ref in other_refs:
                folded = ref[...].astype(F32)
                grad = grad + (folded[:own] if low == 0 else folded[own:, : high - low])
            for c in range(g.cols):
                valid = max(0, min(high, units - c * share) - low)

                @pl.when(pos[2] == c)
                def _():
                    if valid:
                        start = c * share + low
                        gate = gate_ref[:, start : start + valid].astype(F32)
                        up = up_ref[:, start : start + valid].astype(F32)
                        squash = 1.0 / (1.0 + jnp.exp(-gate))
                        base = grad[:, :valid] * squash
                        out_ref[:own, low : low + valid] = (base * up * (1.0 + gate * (1.0 - squash))).astype(BF)
                        out_ref[own:, low : low + valid] = (base * gate).astype(BF)
                    if valid < high - low:
                        out_ref[:, low + valid : high] = jnp.zeros((2 * own, high - low - valid), BF)

    shape = jax.ShapeDtypeStruct((2 * own, share), BF)
    return local_call(
        kernel, shape, [SM] + [VM] * (len(others) + 3),
        (at, total, *others, gate_pre, up_pre), 6, busy=HINT,
    )


def input_matmul(g, at, pieces, route, img_count, w_gate, w_up, own):
    share = pieces[0].shape[1]
    units, width = w_gate.shape
    slots = route.shape[1]
    image = slots // g.rows
    half = slots // CORES
    rows = len(pieces) // g.cols
    order = [(core, dx, dy) for core in range(CORES) for dx, dy in g.shifts]

    def kernel(pos, count_ref, *refs):
        piece_refs, (route_ref, gate_ref, up_ref, out_ref, left) = refs[: len(pieces)], refs[len(pieces) :]
        for (core, dx, dy), ref in zip(order, piece_refs):
            at_row = (core * g.xs + dx) * 2 * own
            left[(pos[2] - dy + g.cols) % g.cols, at_row : at_row + 2 * own] = ref[...]
        gate, up = 0.0, 0.0
        for c in range(g.cols):
            valid = max(0, min(share, units - c * share))
            for off, n in spans(valid, 1920):
                row = c * share + off
                part = left[c, :, off : off + n]
                gate = gate + dot_nn(part, gate_ref[row : row + n])
                up = up + dot_nn(part, up_ref[row : row + n])
        both = [gate[2 * r * own : 2 * r * own + own] + up[2 * r * own + own : 2 * (r + 1) * own] for r in range(rows)]
        line = route_ref[...]
        device, local = lax.div(line, own), lax.rem(line, own)
        x, core = lax.div(device, CORES), lax.rem(device, CORES)
        away = lax.rem(pos[1] - x + g.xs, g.xs)
        place = (lax.rem(core + pos[0], CORES) * g.xs + away) * own + local
        slot = lax.broadcasted_iota(jnp.int32, (1, slots), 1)
        live = jnp.zeros((1, slots), jnp.int32)
        for r in range(g.rows):
            live = jnp.where(lax.div(slot, image) == r, count_ref[r], live)
        place = jnp.where(lax.rem(slot, image) < live, place, -1)
        pick = jnp.where(lax.broadcasted_iota(jnp.int32, (slots, slots), 0) == place, 1.0, 0.0).astype(BF)
        done = dot_tn(pick, jnp.concatenate(both).astype(BF)).astype(BF)
        for k in range(CORES):

            @pl.when(pos[0] == k)
            def _():
                out_ref[:half] = done[k * half : (k + 1) * half]
                out_ref[half:] = done[(1 - k) * half : (2 - k) * half]

    return local_call(
        kernel, jax.ShapeDtypeStruct((slots, width), BF), [SM, SM] + [VM] * (len(pieces) + 3),
        (at, img_count, *pieces, route, w_gate, w_up), 8,
        [pltpu.VMEM((g.cols, 2 * own * rows, share), BF)],
        busy=(8 * slots * units * width, 4 * units * width),
    )


def fetch_rows(at, w_proj, steps, start, count):
    block = SHUF * LANES
    last = cdiv(w_proj.shape[0], block) - 1

    def kernel(pos, w_ref, out_ref, sem):
        copies = []
        for i in range(count):
            first = jnp.minimum(pos[3] * steps + start + i, last) * block
            copies.append(pltpu.make_async_copy(w_ref.at[pl.ds(first, block)], out_ref.at[i], sem.at[i]))
            copies[-1].start()
        for copy in copies:
            copy.wait()

    shape = jax.ShapeDtypeStruct((count, block, w_proj.shape[1]), BF)
    return local_call(
        kernel, shape, [SM, HBM], (at, in_hbm(w_proj)), 22, [pltpu.SemaphoreType.DMA((count,))],
        busy=(0, 2 * count * block * w_proj.shape[1]),
    )


def shuffle_matmul(g, image_grad, w_parts):
    slots, width = image_grad.shape
    half = slots // CORES
    block, width = w_parts[0].shape[1:]
    steps = sum(w.shape[0] for w in w_parts)
    sub = g.chips // SHUF
    piece = half // sub

    def kernel(grad_ref, *refs):
        w_refs, (keep_ref, give_ref, parts) = refs[: len(w_parts)], refs[len(w_parts) :]
        blocks = [(ref, n) for ref in w_refs for n in range(ref.shape[0])]
        source = lax.broadcasted_iota(jnp.int32, (block, block), 0)
        target = lax.broadcasted_iota(jnp.int32, (block, block), 1)
        order = jnp.where(source == SHUF * (target % LANES) + target // LANES, 1.0, 0.0).astype(BF)
        for i, (ref, n) in enumerate(blocks):
            parts[i * slots : (i + 1) * slots] = dot_nt(grad_ref[...], ref[n]).astype(BF)
        done = dot_nn(parts[...], order).astype(BF)
        for i in range(steps):
            for ref, top in ((keep_ref, i * slots), (give_ref, i * slots + half)):
                for q in range(SHUF):
                    for s in range(sub):
                        rows = done[top + s * piece : top + (s + 1) * piece, q * LANES : (q + 1) * LANES]
                        ref[q * sub + s, :, i * LANES : (i + 1) * LANES] = rows

    shape = jax.ShapeDtypeStruct((g.chips, piece, steps * LANES), BF)
    return local_call(
        kernel, [shape, shape], [VM] * (1 + len(w_parts)), (image_grad, *w_parts), 8,
        [pltpu.VMEM((steps * slots, block), BF)],
        busy=(2 * slots * width * block * steps, 2 * width * block * steps),
    )


def chip_sum(g, at, keep, other):
    def kernel(pos, keep_ref, other_ref, own_ref, *piece_refs):
        for (dx, dy), ref in zip(g.shifts, (own_ref,) + piece_refs):
            chip = (pos[1] + dx) % g.xs * g.cols + (pos[2] + dy) % g.cols
            ref[...] = (keep_ref[chip].astype(F32) + other_ref[chip].astype(F32)).astype(ref.dtype)

    shapes = [jax.ShapeDtypeStruct(keep.shape[1:], F32 if s == (0, 0) else BF) for s in g.shifts]
    return local_call(kernel, shapes, [SM, VM, VM], (at, keep, other), 4)


def order_hidden(g, at, parts, piece):
    group, units = parts[0].shape[1:]
    patches = group * g.rows
    half = patches // (CORES * SHUF)
    masks = row_masks(g)

    def kernel(pos, *refs):
        spot = lax.broadcasted_iota(jnp.int32, (patches, group), 0)
        inner = lax.rem(spot, piece)
        shift = lax.rem(lax.div(spot, piece), g.chips)
        core = lax.rem(lax.div(spot, g.chips * piece) + pos[0], CORES)
        x = lax.rem(pos[1] - lax.div(shift, g.cols) + g.xs, g.xs)
        y = lax.rem(pos[2] - lax.rem(shift, g.cols) + g.cols, g.cols)
        inner = (x * g.cols + y) * piece + inner
        patch = (core * half + lax.rem(inner, half)) * SHUF + lax.div(inner, half)
        source = lax.broadcasted_iota(jnp.int32, (patches, group), 1)
        total, i = 0.0, 0
        for ref in refs[:-1]:
            for part in range(ref.shape[0]):
                row = i if masks is None else masks[i] ^ pos[3]
                pick = jnp.where(patch == source + row * group, 1.0, 0.0).astype(BF)
                total = total + lax.dot_general(
                    ref[part], pick, (((0,), (1,)), ((), ())), preferred_element_type=F32
                )
                i += 1
        refs[-1][...] = total.astype(BF)

    shape = jax.ShapeDtypeStruct((units, patches), BF)
    return local_call(kernel, shape, [SM] + [VM] * len(parts), (at, *parts), 8, busy=(2 * units * patches * patches, 0))


def weight_grad(g, at, result, features, first, pieces, hidden):
    units, patches = hidden.shape
    count, piece, wide = pieces[0].shape
    scale = 1.0 / math.sqrt(patches)
    masks = row_masks(g)
    full, tail = divmod(features, wide)
    parts = spans(wide, 2 * cdiv(wide, 4 * LANES) * LANES)
    fresh = result is None

    def kernel(pos, *refs):
        refs = refs if fresh else refs[1:]
        piece_refs, (hidden_ref, out_ref, patch, buf, sem) = refs[:-5], refs[-5:]
        sends = []
        for i in range(count):
            row = first + i if masks is None else masks[first + i] ^ pos[3]
            for n, ref in enumerate(piece_refs):
                patch[i, n * piece : (n + 1) * piece] = ref[i]
            for n, (off, size) in enumerate(parts):
                buf[i, :, off : off + size] = (dot_nn(hidden_ref[...], patch[i, :, off : off + size]) * scale).astype(BF)
                done = sem.at[i * len(parts) + n]
                begun = []
                if masks is not None or row < full:
                    ends = out_ref.at[:, pl.ds(row * wide + off, size)]
                    begun.append((row < full, pltpu.make_async_copy(buf.at[i, :, pl.ds(off, size)], ends, done)))
                rest = min(size, tail - off)
                if rest > 0:
                    ends = out_ref.at[:, pl.ds(full * wide + off, rest)]
                    begun.append((row == full, pltpu.make_async_copy(buf.at[i, :, pl.ds(off, rest)], ends, done)))
                for now, copy in begun:
                    pl.when(now)(copy.start)
                sends += begun
        for now, copy in sends:
            pl.when(now)(copy.wait)

    return pl.pallas_call(
        kernel,
        out_shape=jax.ShapeDtypeStruct((units, features), BF),
        in_specs=[SM] + ([] if fresh else [HBM]) + [VM] * (len(pieces) + 1),
        out_specs=HBM,
        scratch_shapes=[
            pltpu.VMEM((count, patches, wide), BF),
            pltpu.VMEM((count, units, wide), BF),
            pltpu.SemaphoreType.DMA((count * len(parts),)),
        ],
        input_output_aliases={} if fresh else {1: 0},
        compiler_params=pltpu.CompilerParams(vmem_limit_bytes=16 * MIB),
        cost_estimate=pl.CostEstimate(
            flops=2 * count * patches * wide * units, bytes_accessed=2 * count * units * wide, transcendentals=0
        ),
        name="weight_grad",
    )(at, *([] if fresh else [result]), *pieces, hidden)


def row_steps(g):
    if g.rows & (g.rows - 1):
        return None
    return [1 << n for n in range(g.rows.bit_length() - 1)]


def row_masks(g):
    steps = row_steps(g)
    if steps is None:
        return None
    masks = [0]
    for step in steps:
        masks = masks + [m ^ step for m in masks]
    return masks


def sum_rows(g, value, beside):
    steps = row_steps(g)
    if steps is None:
        return lax.psum(value.astype(F32), "row").astype(BF), beside
    beside = list(beside)
    for n, step in enumerate(steps):
        other = g.send(value, row=lambda r: r ^ step)
        if n < len(beside):
            other, beside[n] = lax.optimization_barrier((other, beside[n]))
        value = (value.astype(F32) + other.astype(F32)).astype(BF)
    return value, beside


def ordered(first, *later):
    return lax.optimization_barrier((first, *later))[1:]


def image_block(out_grad, gate_pre, up_pre, w_gate, w_up, w_down, w_proj, enc_hidden, route, img_count):
    g = Grid()
    at = g.place()
    slots = route.shape[0]
    own = gate_pre.shape[0]
    half = slots // CORES
    units = w_down.shape[0]
    tall = own
    share = cdiv(cdiv(units, g.cols), LANES) * LANES
    steps = row_steps(g)
    doubling = steps is not None

    def to_chips(pieces):
        out = []
        for p, (dx, dy) in zip(pieces, g.shifts[1:]):
            out.append(g.send(p, dx=dx, dy=dy))
        return out

    saved = enc_hidden[None]
    keep, give = down_matmul(g, at, out_grad, w_down, own, tall, share)
    total, *pieces = core_sum(g, at, keep, g.swap(give), tall)
    saved_parts = [saved]
    if steps:
        (mine,) = ordered(total, saved)
        saved_parts.append(g.send(mine, row=lambda r: r ^ steps[0]))
        total, *pieces = lax.optimization_barrier((total, *pieces))
    arrived = to_chips(pieces)
    if steps:
        saved_parts[1], *arrived = lax.optimization_barrier((saved_parts[1], *arrived))
    grads = gate_grads(g, at, total, arrived, gate_pre, up_pre)
    for step in steps[1:] if steps else ():
        (mine,) = ordered(grads, jnp.concatenate(saved_parts))
        saved_parts.append(g.send(mine, row=lambda r: r ^ step))
    pieces = [grads] + to_chips([grads] * (g.chips - 1))
    swapped = [g.swap(grads)]
    pieces = pieces + swapped + [g.swap(p) for p in pieces[1:]]
    if not doubling:
        saved_parts = [lax.all_gather(enc_hidden, "row", axis=0, tiled=False)]
    image_grad = input_matmul(g, at, pieces, route.reshape(1, slots), img_count, w_gate.T, w_up.T, own)

    features = w_proj.shape[0] // SHUF
    lanes = cdiv(cdiv(features, g.rows), LANES)
    piece = SHUF * half // g.chips
    image_grad, late = lax.optimization_barrier((image_grad, at))
    early = lanes // 2 + 1
    w_parts = [fetch_rows(late, w_proj, lanes, s, n) for s, n in ((0, early), (early, lanes - early)) if n]
    image_grad, w_parts = sum_rows(g, image_grad, w_parts)

    keep, give = shuffle_matmul(g, image_grad, w_parts)
    total, *pieces = chip_sum(g, at, keep, g.swap(give))
    for part in to_chips(pieces):
        total = total + part.astype(F32)
    patch_grad = total.astype(BF)
    late, patch_grad = lax.optimization_barrier((at, patch_grad))
    hidden = order_hidden(g, late, saved_parts, piece)

    if not doubling:
        batches = [lax.all_gather(patch_grad, "row", axis=0, tiled=False)]
    else:
        stack, batches = patch_grad[None], []
        for n, step in enumerate(steps):
            other = g.send(stack, row=lambda r: r ^ step)
            if n == 0:
                other, hidden = lax.optimization_barrier((other, hidden))
            stack = jnp.concatenate([stack, other])
            batches.append(stack if n == 0 else other)
        batches = batches or [stack]
    result, first = None, 0
    held = []
    for batch in batches:
        held.append([batch] + to_chips([batch] * (g.chips - 1)))
    for batch, pieces in zip(batches, held):
        if result is not None:
            result, *pieces = lax.optimization_barrier((result, *pieces))
        others = [g.swap(batch)]
        others += [g.swap(p) for p in pieces[1:]]
        result = weight_grad(g, at, result, features, first, pieces + others, hidden)
        first += batch.shape[0]
    return result.T


def solution(mesh):
    placed = (
        P(None, ("enc", "col")),
        P("enc", "row"),
        P("enc", "row"),
        P(("enc", "col"), "row"),
        P(("enc", "col"), "row"),
        P("row", ("enc", "col")),
        P(None, ("enc", "col")),
        P("row", ("enc", "col")),
        P(),
        P(),
    )
    return jax.shard_map(image_block, mesh=mesh, in_specs=placed, out_specs=P(None, ("enc", "col")), check_vma=False)
```

```python
import math

import jax
import jax.numpy as jnp
from jax import lax
from jax.experimental import pallas as pl
from jax.experimental.pallas import tpu as pltpu
from jax.sharding import PartitionSpec as P

SHUF = 4
CORES = 2
LANES = 128
AXES = ("enc", "row", "col")
BF = jnp.bfloat16
F32 = jnp.float32


def cdiv(a, b):
    return -(-a // b)


def dot_nt(left, right):
    return lax.dot_general(left, right, (((1,), (1,)), ((), ())), preferred_element_type=F32)


def dot_nn(left, right):
    return lax.dot_general(left, right, (((1,), (0,)), ((), ())), preferred_element_type=F32)


def dot_tn(left, right):
    return lax.dot_general(left, right, (((0,), (0,)), ((), ())), preferred_element_type=F32)


class Grid:
    def __init__(self):
        self.enc, self.rows, self.cols = (lax.axis_size(a) for a in AXES)
        self.xs = self.enc // CORES
        self.chips = self.xs * self.cols
        enc = lax.axis_index("enc")
        self.core = enc % CORES
        self.x = enc // CORES
        self.y = lax.axis_index("col")
        self.z = lax.axis_index("row")
        self.shifts = [(dx, dy) for dx in range(self.xs) for dy in range(self.cols)]

    def send(self, value, dx=0, dy=0, core=0, row=None):
        pairs = []
        for e in range(self.enc):
            for r in range(self.rows):
                for c in range(self.cols):
                    x, k = divmod(e, CORES)
                    target = (((x + dx) % self.xs) * CORES + (k ^ core), r if row is None else row(r), (c + dy) % self.cols)
                    flat = [(a * self.rows + b) * self.cols + d for a, b, d in ((e, r, c), target)]
                    pairs.append(tuple(flat))
        return lax.ppermute(value, AXES, pairs)

    def swap(self, value):
        return self.send(value, core=1)

    def place(self):
        return jnp.stack([self.core, self.x, self.y, self.z]).astype(jnp.int32)


MIB = 2**20
HINT = (4 * 10**10, 10**8)
VM = pl.BlockSpec(memory_space=pltpu.VMEM)
SM = pl.BlockSpec(memory_space=pltpu.SMEM)
HBM = pl.BlockSpec(memory_space=pltpu.HBM)


def local_call(kernel, out_shape, in_specs, args, limit, scratch=(), busy=(0, 0), out_specs=None):
    return pl.pallas_call(
        kernel,
        out_shape=out_shape,
        in_specs=in_specs,
        out_specs=jax.tree.map(lambda _: VM, out_shape) if out_specs is None else out_specs,
        scratch_shapes=list(scratch),
        compiler_params=pltpu.CompilerParams(vmem_limit_bytes=limit * MIB),
        cost_estimate=pl.CostEstimate(flops=busy[0], bytes_accessed=busy[1], transcendentals=0),
    )(*args)


def in_hbm(value):
    return pltpu.with_memory_space_constraint(value, pltpu.HBM)


def spans(total, step):
    return [(s, min(step, total - s)) for s in range(0, total, step)]


def down_matmul(g, at, out_grad, w_down, own, tall, share):
    slots, width = out_grad.shape
    units = w_down.shape[0]
    half = g.xs * tall
    parts = []
    for c in range(g.cols):
        valid = max(0, min(share, units - c * share))
        parts += [(c, off, n) for off, n in spans(valid, 2048)]

    def kernel(pos, grad_hbm, w_ref, keep_ref, give_ref, grad_ref, buf, sem):
        first = pltpu.make_async_copy(grad_hbm, grad_ref, sem.at[len(parts)])
        first.start()
        copies = []
        for i, (c, off, n) in enumerate(parts):
            span = pl.ds(c * share + off, n)
            copies.append(pltpu.make_async_copy(w_ref.at[span], buf.at[span], sem.at[i]))
            copies[-1].start()
        row = lax.broadcasted_iota(jnp.int32, (CORES * half, slots), 0)
        col = lax.broadcasted_iota(jnp.int32, (CORES * half, slots), 1)
        core, x, inner = row // half, row // tall % g.xs, row % tall
        device = (x + pos[1]) % g.xs * CORES + (core + pos[0]) % CORES
        pick = jnp.where((inner < own) & (col == device * own + inner), 1.0, 0.0).astype(BF)
        first.wait()
        left = dot_nn(pick, grad_ref[...]).astype(BF)
        for copy, (c, off, n) in zip(copies, parts):
            copy.wait()
            out = dot_nt(left, buf[c * share + off : c * share + off + n]).astype(BF)
            keep_ref[c, :, off : off + n] = out[:half]
            give_ref[c, :, off : off + n] = out[half:]
        for c in range(g.cols):
            valid = max(0, min(share, units - c * share))
            if valid < share:
                for ref in (keep_ref, give_ref):
                    ref[c, :, valid:] = jnp.zeros((half, share - valid), BF)

    shape = jax.ShapeDtypeStruct((g.cols, half, share), BF)
    return local_call(
        kernel, [shape, shape], [SM, HBM, HBM], (at, in_hbm(out_grad), in_hbm(w_down)), 52,
        [pltpu.VMEM((slots, width), BF), pltpu.VMEM((units, width), BF), pltpu.SemaphoreType.DMA((len(parts) + 1,))],
        busy=(2 * slots * units * width, 2 * units * width),
    )


def core_sum(g, at, keep, other, tall):
    share = keep.shape[2]
    fold = cdiv(share // LANES, 2) * LANES

    def kernel(pos, keep_ref, other_ref, own_ref, *piece_refs):
        for (dx, dy), ref in zip(g.shifts, (own_ref,) + piece_refs):
            col = (pos[2] + dy) % g.cols
            both = keep_ref[col].astype(F32) + other_ref[col].astype(F32)
            part = both[dx * tall : (dx + 1) * tall]
            if (dx, dy) == (0, 0):
                ref[...] = part
            else:
                ref[:tall] = part[:, :fold].astype(BF)
                ref[tall:, : share - fold] = part[:, fold:].astype(BF)
                if share < 2 * fold:
                    ref[tall:, share - fold :] = jnp.zeros((tall, 2 * fold - share), BF)

    shapes = [
        jax.ShapeDtypeStruct((tall, share), F32) if s == (0, 0) else jax.ShapeDtypeStruct((2 * tall, fold), BF)
        for s in g.shifts
    ]
    return local_call(kernel, shapes, [SM, VM, VM], (at, keep, other), 4, busy=HINT)


def gate_grads(g, at, total, others, gate_pre, up_pre):
    own, units = gate_pre.shape
    share = total.shape[1]
    fold = cdiv(share // LANES, 2) * LANES

    def kernel(pos, total_ref, *refs):
        other_refs, (gate_ref, up_ref, out_ref) = refs[:-3], refs[-3:]
        for low, high in ((0, fold), (fold, share)):
            grad = total_ref[:, low:high]
            for ref in other_refs:
                folded = ref[...].astype(F32)
                grad = grad + (folded[:own] if low == 0 else folded[own:, : high - low])
            for c in range(g.cols):
                valid = max(0, min(high, units - c * share) - low)

                @pl.when(pos[2] == c)
                def _():
                    if valid:
                        start = c * share + low
                        gate = gate_ref[:, start : start + valid].astype(F32)
                        up = up_ref[:, start : start + valid].astype(F32)
                        squash = 1.0 / (1.0 + jnp.exp(-gate))
                        base = grad[:, :valid] * squash
                        out_ref[:own, low : low + valid] = (base * up * (1.0 + gate * (1.0 - squash))).astype(BF)
                        out_ref[own:, low : low + valid] = (base * gate).astype(BF)
                    if valid < high - low:
                        out_ref[:, low + valid : high] = jnp.zeros((2 * own, high - low - valid), BF)

    shape = jax.ShapeDtypeStruct((2 * own, share), BF)
    return local_call(
        kernel, shape, [SM] + [VM] * (len(others) + 3),
        (at, total, *others, gate_pre, up_pre), 6, busy=HINT,
    )


def input_matmul(g, at, pieces, route, img_count, w_gate, w_up, own):
    share = pieces[0].shape[1]
    units, width = w_gate.shape
    slots = route.shape[1]
    image = slots // g.rows
    half = slots // CORES
    rows = len(pieces) // g.cols
    order = [(core, dx, dy) for core in range(CORES) for dx, dy in g.shifts]

    def kernel(pos, count_ref, *refs):
        piece_refs, (route_ref, gate_ref, up_ref, out_ref, left) = refs[: len(pieces)], refs[len(pieces) :]
        for (core, dx, dy), ref in zip(order, piece_refs):
            at_row = (core * g.xs + dx) * 2 * own
            left[(pos[2] - dy + g.cols) % g.cols, at_row : at_row + 2 * own] = ref[...]
        gate, up = 0.0, 0.0
        for c in range(g.cols):
            valid = max(0, min(share, units - c * share))
            for off, n in spans(valid, 1920):
                row = c * share + off
                part = left[c, :, off : off + n]
                gate = gate + dot_nn(part, gate_ref[row : row + n])
                up = up + dot_nn(part, up_ref[row : row + n])
        both = [gate[2 * r * own : 2 * r * own + own] + up[2 * r * own + own : 2 * (r + 1) * own] for r in range(rows)]
        line = route_ref[...]
        device, local = lax.div(line, own), lax.rem(line, own)
        x, core = lax.div(device, CORES), lax.rem(device, CORES)
        away = lax.rem(pos[1] - x + g.xs, g.xs)
        place = (lax.rem(core + pos[0], CORES) * g.xs + away) * own + local
        slot = lax.broadcasted_iota(jnp.int32, (1, slots), 1)
        live = jnp.zeros((1, slots), jnp.int32)
        for r in range(g.rows):
            live = jnp.where(lax.div(slot, image) == r, count_ref[r], live)
        place = jnp.where(lax.rem(slot, image) < live, place, -1)
        pick = jnp.where(lax.broadcasted_iota(jnp.int32, (slots, slots), 0) == place, 1.0, 0.0).astype(BF)
        done = dot_tn(pick, jnp.concatenate(both).astype(BF)).astype(BF)
        for k in range(CORES):

            @pl.when(pos[0] == k)
            def _():
                out_ref[:half] = done[k * half : (k + 1) * half]
                out_ref[half:] = done[(1 - k) * half : (2 - k) * half]

    return local_call(
        kernel, jax.ShapeDtypeStruct((slots, width), BF), [SM, SM] + [VM] * (len(pieces) + 3),
        (at, img_count, *pieces, route, w_gate, w_up), 8,
        [pltpu.VMEM((g.cols, 2 * own * rows, share), BF)],
        busy=(8 * slots * units * width, 4 * units * width),
    )


def fetch_rows(at, w_proj, steps, start, count):
    block = SHUF * LANES
    last = cdiv(w_proj.shape[0], block) - 1

    def kernel(pos, w_ref, out_ref, sem):
        copies = []
        for i in range(count):
            first = jnp.minimum(pos[3] * steps + start + i, last) * block
            copies.append(pltpu.make_async_copy(w_ref.at[pl.ds(first, block)], out_ref.at[i], sem.at[i]))
            copies[-1].start()
        for copy in copies:
            copy.wait()

    shape = jax.ShapeDtypeStruct((count, block, w_proj.shape[1]), BF)
    return local_call(
        kernel, shape, [SM, HBM], (at, in_hbm(w_proj)), 22, [pltpu.SemaphoreType.DMA((count,))],
        busy=(0, 2 * count * block * w_proj.shape[1]),
    )


def shuffle_matmul(g, image_grad, w_parts):
    slots, width = image_grad.shape
    half = slots // CORES
    block, width = w_parts[0].shape[1:]
    steps = sum(w.shape[0] for w in w_parts)
    sub = g.chips // SHUF
    piece = half // sub

    def kernel(grad_ref, *refs):
        w_refs, (keep_ref, give_ref, parts) = refs[: len(w_parts)], refs[len(w_parts) :]
        blocks = [(ref, n) for ref in w_refs for n in range(ref.shape[0])]
        source = lax.broadcasted_iota(jnp.int32, (block, block), 0)
        target = lax.broadcasted_iota(jnp.int32, (block, block), 1)
        order = jnp.where(source == SHUF * (target % LANES) + target // LANES, 1.0, 0.0).astype(BF)
        for i, (ref, n) in enumerate(blocks):
            parts[i * slots : (i + 1) * slots] = dot_nt(grad_ref[...], ref[n]).astype(BF)
        done = dot_nn(parts[...], order).astype(BF)
        for i in range(steps):
            for ref, top in ((keep_ref, i * slots), (give_ref, i * slots + half)):
                for q in range(SHUF):
                    for s in range(sub):
                        rows = done[top + s * piece : top + (s + 1) * piece, q * LANES : (q + 1) * LANES]
                        ref[q * sub + s, :, i * LANES : (i + 1) * LANES] = rows

    shape = jax.ShapeDtypeStruct((g.chips, piece, steps * LANES), BF)
    return local_call(
        kernel, [shape, shape], [VM] * (1 + len(w_parts)), (image_grad, *w_parts), 8,
        [pltpu.VMEM((steps * slots, block), BF)],
        busy=(2 * slots * width * block * steps, 2 * width * block * steps),
    )


def chip_sum(g, at, keep, other):
    def kernel(pos, keep_ref, other_ref, own_ref, *piece_refs):
        for (dx, dy), ref in zip(g.shifts, (own_ref,) + piece_refs):
            chip = (pos[1] + dx) % g.xs * g.cols + (pos[2] + dy) % g.cols
            ref[...] = (keep_ref[chip].astype(F32) + other_ref[chip].astype(F32)).astype(ref.dtype)

    shapes = [jax.ShapeDtypeStruct(keep.shape[1:], F32 if s == (0, 0) else BF) for s in g.shifts]
    return local_call(kernel, shapes, [SM, VM, VM], (at, keep, other), 4)


def order_hidden(g, at, parts, piece):
    group, units = parts[0].shape[1:]
    patches = group * g.rows
    half = patches // (CORES * SHUF)
    masks = row_masks(g)

    def kernel(pos, *refs):
        spot = lax.broadcasted_iota(jnp.int32, (patches, group), 0)
        inner = lax.rem(spot, piece)
        shift = lax.rem(lax.div(spot, piece), g.chips)
        core = lax.rem(lax.div(spot, g.chips * piece) + pos[0], CORES)
        x = lax.rem(pos[1] - lax.div(shift, g.cols) + g.xs, g.xs)
        y = lax.rem(pos[2] - lax.rem(shift, g.cols) + g.cols, g.cols)
        inner = (x * g.cols + y) * piece + inner
        patch = (core * half + lax.rem(inner, half)) * SHUF + lax.div(inner, half)
        source = lax.broadcasted_iota(jnp.int32, (patches, group), 1)
        total, i = 0.0, 0
        for ref in refs[:-1]:
            for part in range(ref.shape[0]):
                row = i if masks is None else masks[i] ^ pos[3]
                pick = jnp.where(patch == source + row * group, 1.0, 0.0).astype(BF)
                total = total + lax.dot_general(
                    ref[part], pick, (((0,), (1,)), ((), ())), preferred_element_type=F32
                )
                i += 1
        refs[-1][...] = total.astype(BF)

    shape = jax.ShapeDtypeStruct((units, patches), BF)
    return local_call(kernel, shape, [SM] + [VM] * len(parts), (at, *parts), 8, busy=(2 * units * patches * patches, 0))


def weight_grad(g, at, result, features, first, pieces, hidden):
    units, patches = hidden.shape
    count, piece, wide = pieces[0].shape
    scale = 1.0 / math.sqrt(patches)
    masks = row_masks(g)
    full, tail = divmod(features, wide)
    parts = spans(wide, 2 * cdiv(wide, 4 * LANES) * LANES)
    fresh = result is None

    def kernel(pos, *refs):
        refs = refs if fresh else refs[1:]
        piece_refs, (hidden_ref, out_ref, patch, buf, sem) = refs[:-5], refs[-5:]
        sends = []
        for i in range(count):
            row = first + i if masks is None else masks[first + i] ^ pos[3]
            for n, ref in enumerate(piece_refs):
                patch[i, n * piece : (n + 1) * piece] = ref[i]
            for n, (off, size) in enumerate(parts):
                buf[i, :, off : off + size] = (dot_nn(hidden_ref[...], patch[i, :, off : off + size]) * scale).astype(BF)
                done = sem.at[i * len(parts) + n]
                begun = []
                if masks is not None or row < full:
                    ends = out_ref.at[:, pl.ds(row * wide + off, size)]
                    begun.append((row < full, pltpu.make_async_copy(buf.at[i, :, pl.ds(off, size)], ends, done)))
                rest = min(size, tail - off)
                if rest > 0:
                    ends = out_ref.at[:, pl.ds(full * wide + off, rest)]
                    begun.append((row == full, pltpu.make_async_copy(buf.at[i, :, pl.ds(off, rest)], ends, done)))
                for now, copy in begun:
                    pl.when(now)(copy.start)
                sends += begun
        for now, copy in sends:
            pl.when(now)(copy.wait)

    return pl.pallas_call(
        kernel,
        out_shape=jax.ShapeDtypeStruct((units, features), BF),
        in_specs=[SM] + ([] if fresh else [HBM]) + [VM] * (len(pieces) + 1),
        out_specs=HBM,
        scratch_shapes=[
            pltpu.VMEM((count, patches, wide), BF),
            pltpu.VMEM((count, units, wide), BF),
            pltpu.SemaphoreType.DMA((count * len(parts),)),
        ],
        input_output_aliases={} if fresh else {1: 0},
        compiler_params=pltpu.CompilerParams(vmem_limit_bytes=16 * MIB),
        cost_estimate=pl.CostEstimate(
            flops=2 * count * patches * wide * units, bytes_accessed=2 * count * units * wide, transcendentals=0
        ),
        name="weight_grad",
    )(at, *([] if fresh else [result]), *pieces, hidden)


def row_steps(g):
    if g.rows & (g.rows - 1):
        return None
    return [1 << n for n in range(g.rows.bit_length() - 1)]


def row_masks(g):
    steps = row_steps(g)
    if steps is None:
        return None
    masks = [0]
    for step in steps:
        masks = masks + [m ^ step for m in masks]
    return masks


def sum_rows(g, value, beside):
    steps = row_steps(g)
    if steps is None:
        return lax.psum(value.astype(F32), "row").astype(BF), beside
    beside = list(beside)
    for n, step in enumerate(steps):
        other = g.send(value, row=lambda r: r ^ step)
        if n < len(beside):
            other, beside[n] = lax.optimization_barrier((other, beside[n]))
        value = (value.astype(F32) + other.astype(F32)).astype(BF)
    return value, beside


def ordered(first, *later):
    return lax.optimization_barrier((first, *later))[1:]


def image_block(out_grad, gate_pre, up_pre, w_gate, w_up, w_down, w_proj, enc_hidden, route, img_count):
    g = Grid()
    at = g.place()
    slots = route.shape[0]
    own = gate_pre.shape[0]
    half = slots // CORES
    units = w_down.shape[0]
    tall = own
    share = cdiv(cdiv(units, g.cols), LANES) * LANES
    steps = row_steps(g)
    doubling = steps is not None

    def to_chips(pieces):
        out = []
        for p, (dx, dy) in zip(pieces, g.shifts[1:]):
            out.append(g.send(p, dx=dx, dy=dy))
        return out

    saved = enc_hidden[None]
    keep, give = down_matmul(g, at, out_grad, w_down, own, tall, share)
    total, *pieces = core_sum(g, at, keep, g.swap(give), tall)
    saved_parts = [saved]
    if steps:
        (mine,) = ordered(give, saved)
        saved_parts.append(g.send(mine, row=lambda r: r ^ steps[0]))
    arrived = to_chips(pieces)
    grads = gate_grads(g, at, total, arrived, gate_pre, up_pre)
    if steps:
        saved_parts[1], grads = lax.optimization_barrier((saved_parts[1], grads))
    for step in steps[1:] if steps else ():
        (mine,) = ordered(grads, jnp.concatenate(saved_parts))
        saved_parts.append(g.send(mine, row=lambda r: r ^ step))
    pieces = [grads] + to_chips([grads] * (g.chips - 1))
    swapped = [g.swap(grads)]
    pieces = pieces + swapped + [g.swap(p) for p in pieces[1:]]
    if not doubling:
        saved_parts = [lax.all_gather(enc_hidden, "row", axis=0, tiled=False)]
    image_grad = input_matmul(g, at, pieces, route.reshape(1, slots), img_count, w_gate.T, w_up.T, own)

    features = w_proj.shape[0] // SHUF
    lanes = cdiv(cdiv(features, g.rows), LANES)
    piece = SHUF * half // g.chips
    image_grad, late = lax.optimization_barrier((image_grad, at))
    early = lanes // 2 + 1
    w_parts = [fetch_rows(late, w_proj, lanes, s, n) for s, n in ((0, early), (early, lanes - early)) if n]
    image_grad, w_parts = sum_rows(g, image_grad, w_parts)

    keep, give = shuffle_matmul(g, image_grad, w_parts)
    total, *pieces = chip_sum(g, at, keep, g.swap(give))
    for part in to_chips(pieces):
        total = total + part.astype(F32)
    patch_grad = total.astype(BF)
    late, patch_grad = lax.optimization_barrier((at, patch_grad))
    hidden = order_hidden(g, late, saved_parts, piece)

    if not doubling:
        batches = [lax.all_gather(patch_grad, "row", axis=0, tiled=False)]
    else:
        stack, batches = patch_grad[None], []
        for n, step in enumerate(steps):
            other = g.send(stack, row=lambda r: r ^ step)
            if n == 0:
                other, hidden = lax.optimization_barrier((other, hidden))
            stack = jnp.concatenate([stack, other])
            batches.append(stack if n == 0 else other)
        batches = batches or [stack]
    result, first = None, 0
    held = []
    for batch in batches:
        held.append([batch] + to_chips([batch] * (g.chips - 1)))
    for batch, pieces in zip(batches, held):
        others = [g.swap(batch)]
        others += [g.swap(p) for p in pieces[1:]]
        result = weight_grad(g, at, result, features, first, pieces + others, hidden)
        first += batch.shape[0]
    return result.T


def solution(mesh):
    placed = (
        P(None, ("enc", "col")),
        P("enc", "row"),
        P("enc", "row"),
        P(("enc", "col"), "row"),
        P(("enc", "col"), "row"),
        P("row", ("enc", "col")),
        P(None, ("enc", "col")),
        P("row", ("enc", "col")),
        P(),
        P(),
    )
    return jax.shard_map(image_block, mesh=mesh, in_specs=placed, out_specs=P(None, ("enc", "col")), check_vma=False)
```
